128 devices in a mesh: chan: 8 (over x_hi, z), strip: 16 (over x_lo, y, core).
Axes of the slice: x: 4 (x_hi: 2, x_lo: 2; x = x_hi * 2 + x_lo), y: 4, z: 4, core: 2. Of those that a mesh axis runs over, the one named last changes fastest.
Arguments:
- image: float32 [8, 2048, 2048], P('chan', 'strip'), may hold values from 0 to 1
- dual_coeffs: bfloat16 [2, 8, 2048, 2048], P(None, 'chan', 'strip'), may hold values from -4 to 4
- block_ids: int32 [8, 512], P('chan', 'strip'), may hold values from 0 to 63, as said below
- block_counts: int32 [8, 16], P('chan', 'strip'), may hold values from 1 to 32, as said below
- block_weights: bfloat16 [8, 512, 32, 128], P('chan', 'strip'), may hold values from 0.25 to 2
- block_data: bfloat16 [8, 2, 512, 32, 128], P('chan', None, 'strip'), may hold values from -6 to 6
Outputs:
- image_new: float32 [8, 2048, 2048], P('chan', 'strip')
- dual_new: bfloat16 [2, 8, 2048, 2048], P(None, 'chan', 'strip')
The draws below stay inside these ranges and needn't reach their ends.
Inputs may be any that keep to these rules, and one draw needn't show every extreme that they name: `block_ids`: the 32 ids of one channel and one pencil are distinct. `block_counts`: some channel and pencil has all 32 slots live.
All inputs are finite; a program needn't handle non-finite values.
Results may differ from the reference program's by a relative error of at most 0.0055.
Values sent between devices are 32-bit elements; how exact they have to be, the bound alone decides.
A program may use at most 64 MiB of HBM per device.

```python
import math
import jax
import jax.numpy as jnp
from jax import lax

PIXELS = 2048
BANKS = 2
ROW_BLOCKS = 64
SLOTS = 32
CHANNELS = 8
PENCIL = 128
BLOCK_ROWS = 32
N_STRIP = 16


def draw_block_ids(key, part):
    key_list = jax.random.split(key, CHANNELS * N_STRIP)

    def single_order(single_key):
        return jax.random.permutation(single_key, ROW_BLOCKS)[:SLOTS]
    orders = jax.vmap(single_order)(key_list)
    return orders.reshape(CHANNELS, N_STRIP * SLOTS).astype(jnp.int32)


def draw_block_counts(key, part):
    counts = jax.random.randint(key, (CHANNELS * N_STRIP,), 1, SLOTS // 2 + 1)
    chosen = jax.random.randint(jax.random.fold_in(key, 7), (), 0, CHANNELS * N_STRIP)
    flattened = counts.at[chosen].set(SLOTS)
    return flattened.reshape(CHANNELS, N_STRIP).astype(jnp.int32)


def levels(rng, shape, cuts, low, top_value):
    def one(position, shards_of):
        steps = jax.random.uniform(jax.random.fold_in(jax.random.fold_in(rng, 6), position), (shards_of,), jnp.float32, low / len(cuts), top_value / len(cuts))
        return jnp.repeat(jnp.exp(steps), shape[position] // shards_of).reshape((-1,) + (1,) * (len(shape) - position - 1))

    factor_of = one(*cuts[0])
    for cut in cuts[1:]:
        factor_of = factor_of * one(*cut)
    return factor_of


def centred(rng, shape, scale, most, cuts=(), held_as=jnp.bfloat16):
    array = jax.random.normal(rng, shape, jnp.float32) * scale
    if len(cuts) > 0:
        array = levels(rng, shape, cuts, -0.22, 0.18) * array
    return jnp.clip(array, min=-most, max=most).astype(held_as)


def setup_inputs(seed: int = 0) -> dict:
    streams_of = jax.random.split(jax.random.key(seed), 7)
    return {
        "image": jnp.clip(1.0 * jax.random.uniform(streams_of[0], (CHANNELS, PIXELS, PIXELS), jnp.float32) ** levels(streams_of[0], (CHANNELS, PIXELS, PIXELS), ((0, 8), (1, 16)), -0.2, 0.2), 0.0, 1.0),
        "dual_coeffs": centred(streams_of[1], (BANKS, CHANNELS, PIXELS, PIXELS), 0.5, 4.0, ((1, 8), (2, 16))),
        "block_ids": draw_block_ids(jax.random.fold_in(streams_of[6], 71), 0),
        "block_counts": draw_block_counts(jax.random.fold_in(streams_of[6], 71), 0),
        "block_weights": jnp.clip(jnp.exp(math.log(2.0) - 2.0794415 * jax.random.uniform(streams_of[4], (CHANNELS, N_STRIP * SLOTS, BLOCK_ROWS, PENCIL), jnp.float32) ** levels(streams_of[4], (CHANNELS, N_STRIP * SLOTS, BLOCK_ROWS, PENCIL), ((0, 8), (1, 16)), -0.2, 0.2)), 0.25, 2.0).astype(jnp.bfloat16),
        "block_data": centred(streams_of[5], (CHANNELS, 2, N_STRIP * SLOTS, BLOCK_ROWS, PENCIL), 1.0, 6.0, ((0, 8), (2, 16))),
    }


root_three = math.sqrt(3.0)
sqrt_two = math.sqrt(2.0)
daub_two = [(1.0 + root_three) / (4.0 * sqrt_two), (3.0 + root_three) / (4.0 * sqrt_two), (3.0 - root_three) / (4.0 * sqrt_two), (1.0 - root_three) / (4.0 * sqrt_two)]
daub_four = [0.2303778133088964, 0.7148465705529155, 0.6308807679298587, -0.0279837694168599, -0.1870348117190931, 0.0308413818355607, 0.0328830116668852, -0.010597401785069]
bank_filters = [daub_two, daub_four]
rim_width = 4
sigma_dual = 0.5
tau_primal = 0.3
shrink_level = 0.5

def high_from_low(low_taps):
    tap_count = len(low_taps)
    return [(-1) ** tap_index * low_taps[tap_count - 1 - tap_index] for tap_index in range(tap_count)]

def analyse_axis(padded, low_taps, which_axis, length):
    tap_count = len(low_taps)
    high_taps = high_from_low(low_taps)
    offset = tap_count // 2 - 1
    even_part = 0.0
    odd_part = 0.0
    for tap_index in range(tap_count):
        start = tap_index - offset + rim_width
        even_part = even_part + low_taps[tap_index] * lax.slice_in_dim(padded, start, start + length, axis=which_axis)
        odd_part = odd_part + high_taps[tap_index] * lax.slice_in_dim(padded, start - 1, start - 1 + length, axis=which_axis)
    parity = lax.broadcasted_iota(jnp.int32, even_part.shape, which_axis) % 2
    return jnp.where(parity == 0, even_part, odd_part)

def synthesise_axis(padded, low_taps, which_axis, length):
    tap_count = len(low_taps)
    high_taps = high_from_low(low_taps)
    offset = tap_count // 2 - 1
    extent = padded.shape[which_axis]
    parity = lax.broadcasted_iota(jnp.int32, padded.shape, which_axis) % 2
    even_terms = jnp.where(parity == 0, padded, 0.0)
    shifted = lax.slice_in_dim(padded, 1, extent, axis=which_axis)
    odd_terms = jnp.where(lax.slice_in_dim(parity, 0, extent - 1, axis=which_axis) == 0, shifted, 0.0)
    result = 0.0
    for tap_index in range(tap_count):
        start = rim_width + offset - tap_index
        result = result + low_taps[tap_index] * lax.slice_in_dim(even_terms, start, start + length, axis=which_axis)
        result = result + high_taps[tap_index] * lax.slice_in_dim(odd_terms, start, start + length, axis=which_axis)
    return result

def analyse_image(padded, low_taps, strip_rows, pixels):
    columns_done = analyse_axis(padded, low_taps, 2, pixels)
    return analyse_axis(columns_done, low_taps, 1, strip_rows)

def synthesise_image(rimmed, low_taps, strip_rows, pixels):
    rows_done = synthesise_axis(rimmed, low_taps, 1, strip_rows)
    padded = jnp.pad(rows_done, ((0, 0), (0, 0), (rim_width, rim_width)))
    return synthesise_axis(padded, low_taps, 2, pixels)

def apply_blocks(grid_real, grid_imag, slot_ids, slot_counts, slot_weights, data_real, data_imag):
    groups, slots = slot_ids.shape
    index_shape = slot_ids[:, :, None, None]
    picked_real = jnp.take_along_axis(grid_real, index_shape, axis=1)
    picked_imag = jnp.take_along_axis(grid_imag, index_shape, axis=1)
    live_slots = (lax.broadcasted_iota(jnp.int32, (groups, slots), 1) < slot_counts).astype(jnp.float32)[:, :, None, None]
    weight_vals = slot_weights.astype(jnp.float32)
    term_real = live_slots * weight_vals * (weight_vals * picked_real - data_real.astype(jnp.float32))
    term_imag = live_slots * weight_vals * (weight_vals * picked_imag - data_imag.astype(jnp.float32))
    group_index = lax.broadcasted_iota(jnp.int32, (groups, slots), 0)
    empty_grid = jnp.zeros(grid_real.shape, jnp.float32)
    return (empty_grid.at[group_index, slot_ids].add(term_real), empty_grid.at[group_index, slot_ids].add(term_imag))

def channel_analysis(plane):
    padded = jnp.pad(plane, ((rim_width, rim_width), (rim_width, rim_width)))[None]
    return jnp.stack([analyse_image(padded, taps, PIXELS, PIXELS)[0] for taps in bank_filters])

def channel_synthesis(planes):
    total = None
    for bank_index in range(len(bank_filters)):
        padded = jnp.pad(planes[bank_index], ((rim_width, rim_width), (0, 0)))[None]
        term = synthesise_image(padded, bank_filters[bank_index], PIXELS, PIXELS)[0]
        total = term if total is None else total + term
    return total

def channel_gradient(inputs):
    plane, slot_ids, slot_counts, slot_weights, slot_data = inputs
    spectrum = jnp.fft.fft2(plane, norm='ortho')

    def arrange(values):
        return values.reshape(ROW_BLOCKS, BLOCK_ROWS, N_STRIP, PENCIL).transpose(2, 0, 1, 3)
    grid_real = arrange(jnp.real(spectrum).astype(jnp.float32))
    grid_imag = arrange(jnp.imag(spectrum).astype(jnp.float32))
    weights = slot_weights.reshape(N_STRIP, SLOTS, BLOCK_ROWS, PENCIL)
    data_real = slot_data[0].reshape(N_STRIP, SLOTS, BLOCK_ROWS, PENCIL)
    data_imag = slot_data[1].reshape(N_STRIP, SLOTS, BLOCK_ROWS, PENCIL)
    placed_real, placed_imag = apply_blocks(grid_real, grid_imag, slot_ids.reshape(N_STRIP, SLOTS), slot_counts[:, None], weights, data_real, data_imag)

    def restore(values):
        return values.transpose(1, 2, 0, 3).reshape(PIXELS, PIXELS)
    residual = restore(placed_real) + 1j * restore(placed_imag)
    return jnp.real(jnp.fft.ifft2(residual, norm='ortho')).astype(plane.dtype)

def reference(image, dual_coeffs, block_ids, block_counts, block_weights, block_data):
    channels = image.shape[0]
    shrink_bound = shrink_level * math.sqrt(channels)
    coeffs = jnp.swapaxes(lax.map(channel_analysis, image), 0, 1)
    trial_dual = dual_coeffs.astype(jnp.float32) + sigma_dual * coeffs
    squares = lax.optimization_barrier(jnp.sum(trial_dual * trial_dual, axis=1))
    factor = shrink_bound / jnp.maximum(jnp.sqrt(squares), shrink_bound)
    dual_new = (trial_dual * factor[:, None]).astype(jnp.bfloat16)
    combined = 2.0 * dual_new.astype(jnp.float32) - dual_coeffs.astype(jnp.float32)
    adjoint = lax.map(channel_synthesis, jnp.swapaxes(combined, 0, 1))
    gradient = lax.map(channel_gradient, (image, block_ids, block_counts, block_weights, block_data))
    image_new = jnp.maximum(image - tau_primal * (gradient + adjoint), 0.0)
    return (image_new, dual_new)
```

```python
import math

import jax
import jax.numpy as jnp
import numpy as np
from jax import lax
from jax.experimental import pallas as pl
from jax.experimental.pallas import tpu as pltpu
from jax.sharding import PartitionSpec as P

MESH = pl.DeviceIdType.MESH
F32, BF16 = jnp.float32, jnp.bfloat16

PIX = 2048
ROWS = 128
STRIPS = 16
RIM = 8
PAD = ROWS + 2 * RIM
BANKS = 2
QUARTER = ROWS // 4

root_three = math.sqrt(3.0)
sqrt_two = math.sqrt(2.0)
daub_two = [
    (1.0 + root_three) / (4.0 * sqrt_two),
    (3.0 + root_three) / (4.0 * sqrt_two),
    (3.0 - root_three) / (4.0 * sqrt_two),
    (1.0 - root_three) / (4.0 * sqrt_two),
]
daub_four = [
    0.2303778133088964,
    0.7148465705529155,
    0.6308807679298587,
    -0.0279837694168599,
    -0.1870348117190931,
    0.0308413818355607,
    0.0328830116668852,
    -0.010597401785069,
]
bank_filters = [daub_two, daub_four]
sigma_dual = 0.5
tau_primal = 0.3
shrink_level = 0.5


def bank_matrix(taps, out_at, out_count, in_at, in_count):
    count = len(taps)
    high = [(-1) ** k * taps[count - 1 - k] for k in range(count)]
    offset = count // 2 - 1
    matrix = np.zeros((out_count, in_count), np.float64)
    for i in range(out_count):
        m = out_at + i
        even = m - m % 2
        for k in range(count):
            n = even + k - offset - in_at
            if 0 <= n < in_count:
                matrix[i, n] = (taps if m % 2 == 0 else high)[k]
    return matrix


def make_constants():
    two_pi = 2.0 * math.pi
    tables = []
    for parity in range(2):
        tile, part, k = np.meshgrid(np.arange(8), np.arange(2), np.arange(64), indexing="ij")
        freq = 128 * tile + 2 * k + parity
        phase = part * (math.pi / 2)
        if parity == 0:
            freq[0, 1, 0] = PIX // 2
            phase = phase.copy()
            phase[0, 1, 0] = 0.0
        freq, phase = freq.reshape(-1), phase.reshape(-1)
        coarse = two_pi * (32 * np.arange(32)[:, None] * freq[None, :] % PIX) / PIX
        fine = two_pi * (np.arange(32)[:, None] * freq[None, :] % PIX) / PIX + phase[None, :]
        tables += [np.cos(coarse), np.sin(coarse), np.cos(fine) / 32.0, np.sin(fine) / 32.0]
    tables = np.stack(tables).astype(np.float32)
    grid = two_pi * (np.arange(512)[:, None] * np.arange(512)[None, :] % 512) / 512
    fourier = np.concatenate([np.cos(grid), np.sin(grid)], axis=1) / 64.0
    twiddle = np.zeros((512, 128), np.float32)
    for u in (1, 2, 3):
        angle = two_pi * (np.arange(512) * u) / PIX
        twiddle[:, 2 * u - 2] = np.cos(angle)
        twiddle[:, 2 * u - 1] = np.sin(angle)
    ana_cols = np.concatenate(
        [bank_matrix(t, 128, 128, 0, 384).T for t in bank_filters], axis=1
    )
    ana_rows = np.stack([sigma_dual * bank_matrix(t, RIM, ROWS, 0, PAD) for t in bank_filters])
    syn_rows = np.stack([bank_matrix(t, 0, PAD, RIM, ROWS).T for t in bank_filters])
    syn_cols = np.concatenate([bank_matrix(t, 0, 384, 128, 128) for t in bank_filters], axis=0)
    as_bf16 = lambda a: np.asarray(a, np.float32).astype(BF16)
    return (
        tables,
        as_bf16(fourier),
        twiddle,
        as_bf16(ana_cols),
        as_bf16(ana_rows),
        as_bf16(syn_rows),
        as_bf16(syn_cols),
    )


def dot(a, b):
    return jnp.dot(a, b, preferred_element_type=F32)


def swap_halves(values):
    tiles = [
        pltpu.roll(values[:, 128 * t : 128 * t + 128], 64, 1)
        for t in range(values.shape[1] // 128)
    ]
    return jnp.concatenate(tiles, axis=1) if len(tiles) > 1 else tiles[0]


def lanes(shape):
    return lax.broadcasted_iota(jnp.int32, shape, len(shape) - 1)


def loop(count, body):
    def step(i, carry):
        body(i)
        return carry

    lax.fori_loop(0, count, step, 0)


def at(i, width):
    return pl.ds(pl.multiple_of(i * width, width), width)


def kernel(
    image_hbm, dual_hbm, ids_ref, counts_ref, weights_hbm, data_hbm,
    tables_hbm, fourier_hbm, twiddle_hbm, ana_cols_hbm, ana_rows_hbm, syn_rows_hbm, syn_cols_hbm,
    image_out, dual_out,
    xpad, xwide, dual, weights, data, tables, fourier, twiddle, ana_cols, ana_rows, syn_rows, syn_cols,
    basis, folded, ysend, yrecv, hsend, hrecv, coeffs, trial, squares, near, far, quarter_sum, other_sum,
    factor, combined, edge_send, edge_recv, synth_wide, adjoint, wd_flat, wd_dense, forward, backward,
    packed, image_new, dual_new,
    local_sem, y_s, y_r, h_s, h_r, halo_s, halo_r, edge_s, edge_r, far_s, far_r, near_s, near_r,
    x_s, x_r, ga_s, ga_r, gb_s, gb_r, out_sem,
):
    me = lax.axis_index("strip")
    chan = lax.axis_index("chan")
    z = chan % 4
    x_hi = chan // 4
    zp, zm, zf = (z + 1) % 4, (z + 3) % 4, (z + 2) % 4
    up = {"chan": x_hi * 4 + zp}
    down = {"chan": x_hi * 4 + zm}
    across = {"chan": (1 - x_hi) * 4 + z}
    before, after = {"strip": (me + 15) % STRIPS}, {"strip": (me + 1) % STRIPS}
    sign = jnp.where(me < 8, 1, -1)

    loads = [
        pltpu.make_async_copy(src, dst, local_sem.at[i])
        for i, (src, dst) in enumerate(
            [
                (image_hbm, xpad.at[RIM : RIM + ROWS]),
                (tables_hbm, tables),
                (ana_cols_hbm, ana_cols),
                (ana_rows_hbm, ana_rows),
                (dual_hbm, dual),
                (weights_hbm, weights),
                (data_hbm, data),
                (fourier_hbm, fourier),
                (twiddle_hbm, twiddle),
                (syn_rows_hbm, syn_rows),
                (syn_cols_hbm, syn_cols),
            ]
        )
    ]
    for load in loads:
        load.start()

    barrier = pltpu.get_barrier_semaphore()
    for k in range(1, STRIPS):
        pl.semaphore_signal(
            barrier, inc=1, device_id={"strip": (me + k) % STRIPS}, device_id_type=MESH
        )
    for peer in (up, down, across):
        pl.semaphore_signal(barrier, inc=1, device_id=peer, device_id_type=MESH)
    pl.semaphore_wait(barrier, STRIPS + 2)

    def remote(src, dst, send, recv, peer):
        return pltpu.make_async_remote_copy(
            src_ref=src, dst_ref=dst, send_sem=send, recv_sem=recv, device_id=peer, device_id_type=MESH
        )

    halos = [
        remote(xpad.at[RIM : 2 * RIM], xpad.at[RIM + ROWS : PAD], halo_s.at[0], halo_r.at[0], before),
        remote(xpad.at[ROWS : RIM + ROWS], xpad.at[0:RIM], halo_s.at[1], halo_r.at[1], after),
    ]
    loads[0].wait()
    for copy in halos:
        copy.start()

    loads[1].wait()
    for parity in range(2):
        def make_basis(i, parity=parity):
            coarse_cos = tables[4 * parity, pl.ds(i, 1), :]
            coarse_sin = tables[4 * parity + 1, pl.ds(i, 1), :]
            block = coarse_cos * tables[4 * parity + 2] - coarse_sin * tables[4 * parity + 3]
            basis[parity, at(i, 32), :] = block.astype(BF16)

        loop(32, make_basis)
    left, right = xpad[RIM : RIM + ROWS, 0:1024], xpad[RIM : RIM + ROWS, 1024:2048]
    folded[0] = (left + right).astype(BF16)
    folded[1] = (left - right).astype(BF16)
    for parity in range(2):
        for pair in range(4):
            tiles = dot(folded[parity], basis[parity, :, 256 * pair : 256 * pair + 256])
            for half in range(2):
                tile = tiles[:, 128 * half : 128 * half + 128]
                p = 2 * pair + half
                ysend[p, :, 128 * parity : 128 * parity + 128] = tile
                if parity == 1:
                    ysend[15 - p, :, 128:256] = tile
    lane = lanes((ROWS, 128))
    edge_lane = (lane == 0) | (lane == 64)
    first = ysend[0, :, 0:128]
    for p in range(7):
        ysend[15 - p, :, 0:128] = jnp.where(edge_lane, ysend[p + 1, :, 0:128], ysend[p, :, 0:128])
    ysend[8, :, 0:128] = jnp.where(
        lane == 0, pltpu.roll(first, 64, 1), jnp.where(lane == 64, 0.0, ysend[7, :, 0:128])
    )
    ysend[0, :, 0:128] = jnp.where(lane == 64, 0.0, first)

    def y_copy(k):
        q = (me + k) % STRIPS
        return remote(ysend.at[q], yrecv.at[at(me, ROWS)], y_s.at[k], y_r.at[k], {"strip": q})

    for k in range(1, STRIPS):
        y_copy(k).start()
    yrecv[at(me, ROWS), :] = ysend[me]

    for copy in halos:
        copy.wait_recv()
    for i in (2, 3, 4):
        loads[i].wait()
    xwide[:, 0:128] = jnp.zeros((PAD, 128), BF16)
    xwide[:, 128 + PIX : 256 + PIX] = jnp.zeros((PAD, 128), BF16)
    row = lax.broadcasted_iota(jnp.int32, (PAD, PIX), 0)
    outside = ((row < RIM) & (me == 0)) | ((row >= RIM + ROWS) & (me == STRIPS - 1))
    xwide[:, 128 : 128 + PIX] = jnp.where(outside, 0.0, xpad[...]).astype(BF16)

    def analyse_columns(t):
        start = pl.multiple_of(t * 128, 128)
        both = dot(xwide[:, pl.ds(start, 384)], ana_cols[...]).astype(BF16)
        coeffs[0, :, pl.ds(start, 128)] = both[:, 0:128]
        coeffs[1, :, pl.ds(start, 128)] = both[:, 128:256]

    loop(16, analyse_columns)

    def far_copies(bank):
        return [
            remote(
                squares.at[bank, pl.ds(pl.multiple_of(zf * QUARTER, QUARTER), 16)],
                far.at[bank, 0], far_s.at[2 * bank], far_r.at[2 * bank], up,
            ),
            remote(
                squares.at[bank, pl.ds(pl.multiple_of(zf * QUARTER + 16, 16), 16)],
                far.at[bank, 1], far_s.at[2 * bank + 1], far_r.at[2 * bank + 1], down,
            ),
        ]

    def near_copies(bank):
        return [
            remote(
                squares.at[bank, at(zp, QUARTER)], near.at[bank, 0],
                near_s.at[2 * bank], near_r.at[2 * bank], up,
            ),
            remote(
                squares.at[bank, at(zm, QUARTER)], near.at[bank, 1],
                near_s.at[2 * bank + 1], near_r.at[2 * bank + 1], down,
            ),
        ]

    def x_copy(bank):
        return remote(quarter_sum.at[bank], other_sum.at[bank], x_s.at[bank], x_r.at[bank], across)

    def gather_near(bank):
        mine = factor.at[bank, at(z, QUARTER)]
        return [
            remote(mine, mine, ga_s.at[2 * bank], ga_r.at[2 * bank], up),
            remote(mine, mine, ga_s.at[2 * bank + 1], ga_r.at[2 * bank + 1], down),
        ]

    def gather_far(bank):
        low = factor.at[bank, pl.ds(pl.multiple_of(zm * QUARTER, QUARTER), 16)]
        high = factor.at[bank, pl.ds(pl.multiple_of(zp * QUARTER + 16, 16), 16)]
        return [
            remote(low, low, gb_s.at[2 * bank], gb_r.at[2 * bank], up),
            remote(high, high, gb_s.at[2 * bank + 1], gb_r.at[2 * bank + 1], down),
        ]

    for bank in range(BANKS):
        def analyse_rows(t, bank=bank):
            cols = at(t, 512)
            values = dual[bank, :, cols].astype(F32) + dot(ana_rows[bank], coeffs[bank, :, cols])
            trial[bank, :, cols] = values
            squares[bank, :, cols] = values * values

        loop(4, analyse_rows)
        for copy in far_copies(bank):
            copy.start()

    for i in (5, 6, 7, 8):
        loads[i].wait()
    lane256 = lanes((128, 256))
    column = 2 * (lane256 % 64) + lane256 // 128
    column = jnp.where(me < 8, column, (128 - column) % 128)
    hit = lax.broadcasted_iota(jnp.int32, (128, 256), 0) == column
    imag_lane = (lane256 // 64) % 2 == 1
    pick_both = jnp.where(hit, 1.0, 0.0).astype(BF16)
    pick_real = jnp.where(hit & ~imag_lane, 1.0, 0.0).astype(BF16)
    pick_imag = (jnp.where(hit & imag_lane, 1.0, 0.0) * sign.astype(F32)).astype(BF16)

    def pick_columns(i):
        rows = at(i, 256)
        blocks = at(i, 8)
        flat = (
            dot(weights[blocks].reshape(256, 128), pick_both),
            dot(data[0, blocks].reshape(256, 128), pick_real)
            + dot(data[1, blocks].reshape(256, 128), pick_imag),
        )
        for kind in range(2):
            for half in range(2):
                wd_flat[2 * kind + half, rows, :] = flat[kind][:, 128 * half : 128 * half + 128]

    loop(4, pick_columns)
    slot = lanes((8, 32))
    live_ids = jnp.where(slot < counts_ref[...], ids_ref[...], -1).astype(F32).astype(BF16)
    spread = jnp.where(
        lanes((32, 256)) // 8 == lax.broadcasted_iota(jnp.int32, (32, 256), 0), 1.0, 0.0
    ).astype(BF16)
    slot_ids = dot(live_ids, spread)[0:1, :].astype(jnp.int32)
    place_row = lax.broadcasted_iota(jnp.int32, (512, 256), 0)
    place_col = lanes((512, 256))
    place = jnp.where(
        (slot_ids == place_row // 8) & (place_row % 8 == place_col % 8), 1.0, 0.0
    ).astype(BF16)
    for kind in range(2):
        for u in range(4):
            picked = jnp.concatenate(
                [
                    wd_flat[2 * kind, pl.ds(u, 256, stride=4), :],
                    wd_flat[2 * kind + 1, pl.ds(u, 256, stride=4), :],
                ],
                axis=1,
            ).astype(BF16)
            wd_dense[kind, u] = dot(place, picked).astype(BF16)

    for bank in range(BANKS):
        for copy in far_copies(bank):
            copy.wait_recv()
        low = pl.ds(pl.multiple_of(zp * QUARTER, QUARTER), 16)
        high = pl.ds(pl.multiple_of(zm * QUARTER + 16, 16), 16)
        squares[bank, low, :] = squares[bank, low, :] + far[bank, 0]
        squares[bank, high, :] = squares[bank, high, :] + far[bank, 1]
        for copy in near_copies(bank):
            copy.start()
    for bank in range(BANKS):
        for copy in near_copies(bank):
            copy.wait_recv()
        quarter_sum[bank] = squares[bank, at(z, QUARTER), :] + near[bank, 0] + near[bank, 1]
        x_copy(bank).start()

    lane_sign = jnp.where((lanes((1, 256)) // 64) % 2 == 0, -sign, sign).astype(F32)
    for k in range(1, STRIPS):
        y_copy(k).wait_recv()

    def fold_rows(i):
        rows = at(i, 64)
        low = pl.ds(pl.multiple_of(512 + i * 64, 64), 64)
        y0, y1, y2, y3 = (
            yrecv[pl.ds(pl.multiple_of(512 * j + i * 64, 64), 64), :] for j in range(4)
        )
        tw = twiddle[rows, :]
        c1, s1, c2, s2, c3, s3 = (tw[:, j : j + 1] for j in range(6))
        sum_a, sum_b, dif_a, dif_b = y0 + y2, y1 + y3, y0 - y2, y1 - y3
        forward[0, rows, 0:256] = (sum_a + sum_b).astype(BF16)
        alt = sum_a - sum_b
        parts = (
            (c1 * dif_a - s1 * dif_b, -c1 * dif_b - s1 * dif_a),
            (c2 * alt, -s2 * alt),
            (c3 * dif_a + s3 * dif_b, c3 * dif_b - s3 * dif_a),
        )
        for u, (real, imag) in enumerate(parts, 1):
            real, imag = real.astype(BF16), imag.astype(BF16)
            forward[u, rows, 0:256] = real
            forward[u, low, 0:256] = imag
            forward[u, rows, 256:512] = imag
            forward[u, low, 256:512] = -real

    loop(8, fold_rows)

    for u in range(4):
        def weigh(m, u=u):
            rows = at(m, 128)
            low = pl.ds(pl.multiple_of(512 + m * 128, 128), 128)
            if u == 0:
                real = dot(fourier[rows, 0:512], forward[0, 0:512, 0:256])
                imag = -dot(fourier[rows, 512:1024], forward[0, 0:512, 0:256])
            else:
                both = dot(fourier[rows, :], forward[u])
                real, imag = both[:, 0:256], both[:, 256:512]
            spectrum = real + lane_sign * swap_halves(imag)
            weight = wd_dense[0, u, rows, :].astype(F32)
            residual = weight * (weight * spectrum - wd_dense[1, u, rows, :].astype(F32))
            turned = (lane_sign * swap_halves(residual)).astype(BF16)
            residual = residual.astype(BF16)
            backward[u, rows, 0:256] = residual
            backward[u, low, 0:256] = turned
            if u > 0:
                backward[u, rows, 256:512] = -turned
                backward[u, low, 256:512] = residual

        loop(4, weigh)

    def unfold_rows(m):
        rows = at(m, 128)
        left_side = fourier[rows, :]
        tw = twiddle[rows, :]
        c1, s1, c2, s2, c3, s3 = (tw[:, j : j + 1] for j in range(6))
        k0 = dot(left_side, backward[0, :, 0:256])
        k1, k2, k3 = (dot(left_side, backward[u]) for u in (1, 2, 3))
        r1 = c1 * k1[:, 0:256] - s1 * k1[:, 256:512]
        i1 = c1 * k1[:, 256:512] + s1 * k1[:, 0:256]
        r2 = c2 * k2[:, 0:256] - s2 * k2[:, 256:512]
        r3 = c3 * k3[:, 0:256] - s3 * k3[:, 256:512]
        i3 = c3 * k3[:, 256:512] + s3 * k3[:, 0:256]
        plus, minus, real, imag = k0 + r2, k0 - r2, r1 + r3, i3 - i1
        for j, value in enumerate((plus + real, minus + imag, plus - real, minus - imag)):
            hsend[pl.ds(pl.multiple_of(512 * j + m * 128, 128), 128), :] = value

    loop(4, unfold_rows)

    def h_copy(k):
        q = (me + k) % STRIPS
        return remote(hsend.at[at(q, ROWS)], hrecv.at[me], h_s.at[k], h_r.at[k], {"strip": q})

    for k in range(1, STRIPS):
        h_copy(k).start()
    hrecv[me] = hsend[at(me, ROWS), :]

    bound = shrink_level * math.sqrt(8.0)
    for bank in range(BANKS):
        x_copy(bank).wait_recv()
        total = quarter_sum[bank] + other_sum[bank]
        factor[bank, at(z, QUARTER), :] = bound / jnp.maximum(jnp.sqrt(total), bound)
        for copy in gather_near(bank):
            copy.start()
    for bank in range(BANKS):
        for copy in gather_near(bank):
            copy.wait_recv()
        for copy in gather_far(bank):
            copy.start()

    dual_outs = []
    for bank in range(BANKS):
        for copy in gather_far(bank):
            copy.wait_recv()

        def shrink(i, bank=bank):
            rows = at(i, 16)
            fresh = (trial[bank, rows, :] * factor[bank, rows, :]).astype(BF16)
            dual_new[bank, rows, :] = fresh
            inner = pl.ds(pl.multiple_of(RIM + i * 16, 8), 16)
            combined[bank, inner, :] = 2.0 * fresh.astype(F32) - dual[bank, rows, :].astype(F32)

        loop(8, shrink)
        edge_send[bank, 0] = combined[bank, RIM : 2 * RIM]
        edge_send[bank, 1] = combined[bank, ROWS : RIM + ROWS]
        for copy in edge_copies(remote, bank, edge_send, edge_recv, edge_s, edge_r, before, after):
            copy.start()
    dual_copy = pltpu.make_async_copy(dual_new, dual_out, out_sem.at[0])
    dual_copy.start()

    for bank in range(BANKS):
        for copy in edge_copies(remote, bank, edge_send, edge_recv, edge_s, edge_r, before, after):
            copy.wait_recv()
        combined[bank, RIM + ROWS : PAD] = jnp.where(me == STRIPS - 1, 0.0, edge_recv[bank, 0])
        combined[bank, 0:RIM] = jnp.where(me == 0, 0.0, edge_recv[bank, 1])
    for i in (9, 10):
        loads[i].wait()
    for bank in range(BANKS):
        synth_wide[bank, :, 0:128] = jnp.zeros((ROWS, 128), BF16)
        synth_wide[bank, :, 128 + PIX : 256 + PIX] = jnp.zeros((ROWS, 128), BF16)

        def synthesise_rows(t, bank=bank):
            values = dot(syn_rows[bank], combined[bank, :, at(t, 512)].astype(BF16))
            synth_wide[bank, :, pl.ds(pl.multiple_of(128 + t * 512, 128), 512)] = values.astype(BF16)

        loop(4, synthesise_rows)

    def synthesise_columns(t):
        start = pl.multiple_of(t * 128, 128)
        window = pl.ds(start, 384)
        adjoint[:, pl.ds(start, 128)] = dot(synth_wide[0, :, window], syn_cols[0:384]) + dot(
            synth_wide[1, :, window], syn_cols[384:768]
        )

    loop(16, synthesise_columns)

    for k in range(1, STRIPS):
        h_copy(k).wait_recv()
    for p in range(8):
        own = hrecv[p, :, 0:128]
        if p == 0:
            even = jnp.where(
                lane == 0, own,
                jnp.where(lane == 64, pltpu.roll(hrecv[8, :, 0:128], 64, 1), own + hrecv[15, :, 0:128]),
            )
        else:
            even = own + jnp.where(edge_lane, hrecv[16 - p, :, 0:128], hrecv[15 - p, :, 0:128])
        odd = hrecv[p, :, 128:256] + hrecv[15 - p, :, 128:256]
        packed[0, :, 128 * p : 128 * p + 128] = even.astype(BF16)
        packed[1, :, 128 * p : 128 * p + 128] = odd.astype(BF16)

    def finish(i):
        cols = at(i, 256)
        turn = (((1,), (1,)), ((), ()))
        even, odd = (
            lax.dot_general(packed[j], basis[j, cols, :], turn, preferred_element_type=F32)
            for j in range(2)
        )
        for gradient, where in (
            (even + odd, cols),
            (even - odd, pl.ds(pl.multiple_of(1024 + i * 256, 256), 256)),
        ):
            image_new[:, where] = jnp.maximum(
                xpad[RIM : RIM + ROWS, where] - tau_primal * (gradient + adjoint[:, where]), 0.0
            )

    loop(4, finish)
    image_copy = pltpu.make_async_copy(image_new, image_out, out_sem.at[1])
    image_copy.start()

    for copy in halos:
        copy.wait_send()
    for k in range(1, STRIPS):
        y_copy(k).wait_send()
        h_copy(k).wait_send()
    for bank in range(BANKS):
        for copy in far_copies(bank) + near_copies(bank) + gather_near(bank) + gather_far(bank):
            copy.wait_send()
        x_copy(bank).wait_send()
        for copy in edge_copies(remote, bank, edge_send, edge_recv, edge_s, edge_r, before, after):
            copy.wait_send()
    dual_copy.wait()
    image_copy.wait()


def edge_copies(remote, bank, edge_send, edge_recv, edge_s, edge_r, before, after):
    return [
        remote(
            edge_send.at[bank, side], edge_recv.at[bank, side],
            edge_s.at[2 * bank + side], edge_r.at[2 * bank + side], (before, after)[side],
        )
        for side in range(2)
    ]


def per_device(constants, image, dual_coeffs, block_ids, block_counts, block_weights, block_data):
    any_space = pl.BlockSpec(memory_space=pl.ANY)
    in_vmem = pl.BlockSpec(memory_space=pltpu.VMEM)
    dma = lambda n: pltpu.SemaphoreType.DMA((n,))
    vmem = pltpu.VMEM
    image_new, dual_new = pl.pallas_call(
        kernel,
        out_shape=(
            jax.ShapeDtypeStruct((ROWS, PIX), F32),
            jax.ShapeDtypeStruct((BANKS, ROWS, PIX), BF16),
        ),
        in_specs=[any_space, any_space, in_vmem, in_vmem] + [any_space] * 9,
        out_specs=(any_space, any_space),
        scratch_shapes=[
            vmem((PAD, PIX), F32),
            vmem((PAD, PIX + 256), BF16),
            vmem((BANKS, ROWS, PIX), BF16),
            vmem((32, 32, 128), BF16),
            vmem((2, 32, 32, 128), BF16),
            vmem((8, 32, 1024), F32),
            vmem((512, 1024), BF16),
            vmem((512, 128), F32),
            vmem((384, 256), BF16),
            vmem((BANKS, ROWS, PAD), BF16),
            vmem((BANKS, ROWS, PAD), BF16),
            vmem((768, 128), BF16),
            vmem((2, 1024, 1024), BF16),
            vmem((2, ROWS, 1024), BF16),
            vmem((STRIPS, ROWS, 256), F32),
            vmem((PIX, 256), F32),
            vmem((PIX, 256), F32),
            vmem((STRIPS, ROWS, 256), F32),
            vmem((BANKS, PAD, PIX), BF16),
            vmem((BANKS, ROWS, PIX), F32),
            vmem((BANKS, ROWS, PIX), F32),
            vmem((BANKS, 2, QUARTER, PIX), F32),
            vmem((BANKS, 2, 16, PIX), F32),
            vmem((BANKS, QUARTER, PIX), F32),
            vmem((BANKS, QUARTER, PIX), F32),
            vmem((BANKS, ROWS, PIX), F32),
            vmem((BANKS, PAD, PIX), F32),
            vmem((BANKS, 2, RIM, PIX), F32),
            vmem((BANKS, 2, RIM, PIX), F32),
            vmem((BANKS, ROWS, PIX + 256), BF16),
            vmem((ROWS, PIX), F32),
            vmem((4, 1024, 128), F32),
            vmem((2, 4, 512, 256), BF16),
            vmem((4, 1024, 512), BF16),
            vmem((4, 1024, 512), BF16),
            vmem((2, ROWS, 1024), BF16),
            vmem((ROWS, PIX), F32),
            vmem((BANKS, ROWS, PIX), BF16),
            dma(11), dma(16), dma(16), dma(16), dma(16), dma(2), dma(2), dma(4), dma(4),
            dma(4), dma(4), dma(4), dma(4), dma(2), dma(2), dma(4), dma(4), dma(4), dma(4), dma(2),
        ],
        compiler_params=pltpu.CompilerParams(
            collective_id=0, has_side_effects=True, vmem_limit_bytes=60 * 1024 * 1024
        ),
    )(
        image[0],
        dual_coeffs[:, 0],
        jnp.broadcast_to(block_ids, (8, 32)),
        jnp.broadcast_to(block_counts, (8, 32)),
        block_weights[0],
        block_data[0],
        *constants,
    )
    return image_new[None], dual_new[:, None]


def solution(mesh):
    constants = tuple(jnp.asarray(c) for c in make_constants())

    def body(*args):
        return per_device(constants, *args)

    return jax.shard_map(
        body,
        mesh=mesh,
        in_specs=(
            P("chan", "strip", None),
            P(None, "chan", "strip", None),
            P("chan", "strip"),
            P("chan", "strip"),
            P("chan", "strip", None, None),
            P("chan", None, "strip", None, None),
        ),
        out_specs=(P("chan", "strip", None), P(None, "chan", "strip", None)),
        check_vma=False,
    )
```

```python
import math

import jax
import jax.numpy as jnp
import numpy as np
from jax import lax
from jax.experimental import pallas as pl
from jax.experimental.pallas import tpu as pltpu
from jax.sharding import PartitionSpec as P

MESH = pl.DeviceIdType.MESH
F32, BF16 = jnp.float32, jnp.bfloat16

PIX = 2048
ROWS = 128
STRIPS = 16
RIM = 8
PAD = ROWS + 2 * RIM
BANKS = 2
QUARTER = ROWS // 4
FAR_FIRST = [
    (dx, dy, core)
    for dx, dy in ((1, 2), (0, 2), (1, 1), (1, 3), (0, 1), (0, 3), (1, 0))
    for core in (0, 1)
] + [(0, 0, 1)]

root_three = math.sqrt(3.0)
sqrt_two = math.sqrt(2.0)
daub_two = [
    (1.0 + root_three) / (4.0 * sqrt_two),
    (3.0 + root_three) / (4.0 * sqrt_two),
    (3.0 - root_three) / (4.0 * sqrt_two),
    (1.0 - root_three) / (4.0 * sqrt_two),
]
daub_four = [
    0.2303778133088964,
    0.7148465705529155,
    0.6308807679298587,
    -0.0279837694168599,
    -0.1870348117190931,
    0.0308413818355607,
    0.0328830116668852,
    -0.010597401785069,
]
bank_filters = [daub_two, daub_four]
sigma_dual = 0.5
tau_primal = 0.3
shrink_level = 0.5


def bank_matrix(taps, out_at, out_count, in_at, in_count):
    count = len(taps)
    high = [(-1) ** k * taps[count - 1 - k] for k in range(count)]
    offset = count // 2 - 1
    matrix = np.zeros((out_count, in_count), np.float64)
    for i in range(out_count):
        m = out_at + i
        even = m - m % 2
        for k in range(count):
            n = even + k - offset - in_at
            if 0 <= n < in_count:
                matrix[i, n] = (taps if m % 2 == 0 else high)[k]
    return matrix


def make_constants():
    two_pi = 2.0 * math.pi
    tables = []
    for parity in range(2):
        tile, part, k = np.meshgrid(np.arange(8), np.arange(2), np.arange(64), indexing="ij")
        freq = 128 * tile + 2 * k + parity
        phase = part * (math.pi / 2)
        if parity == 0:
            freq[0, 1, 0] = PIX // 2
            phase = phase.copy()
            phase[0, 1, 0] = 0.0
        freq, phase = freq.reshape(-1), phase.reshape(-1)
        coarse = two_pi * (32 * np.arange(32)[:, None] * freq[None, :] % PIX) / PIX
        fine = two_pi * (np.arange(32)[:, None] * freq[None, :] % PIX) / PIX + phase[None, :]
        tables += [np.cos(coarse), np.sin(coarse), np.cos(fine) / 32.0, np.sin(fine) / 32.0]
    tables = np.stack(tables).astype(np.float32)
    grid = two_pi * (np.arange(512)[:, None] * np.arange(512)[None, :] % 512) / 512
    fourier = np.concatenate([np.cos(grid), np.sin(grid)], axis=1) / 64.0
    twiddle = np.zeros((512, 128), np.float32)
    for u in (1, 2, 3):
        angle = two_pi * (np.arange(512) * u) / PIX
        twiddle[:, 2 * u - 2] = np.cos(angle)
        twiddle[:, 2 * u - 1] = np.sin(angle)
    ana_cols = np.concatenate(
        [bank_matrix(t, 128, 128, 0, 384).T for t in bank_filters], axis=1
    )
    ana_rows = np.stack([sigma_dual * bank_matrix(t, RIM, ROWS, 0, PAD) for t in bank_filters])
    syn_rows = np.stack([bank_matrix(t, 0, PAD, RIM, ROWS).T for t in bank_filters])
    syn_cols = np.concatenate([bank_matrix(t, 0, 384, 128, 128) for t in bank_filters], axis=0)
    as_bf16 = lambda a: np.asarray(a, np.float32).astype(BF16)
    return (
        tables,
        as_bf16(fourier),
        twiddle,
        as_bf16(ana_cols),
        as_bf16(ana_rows),
        as_bf16(syn_rows),
        as_bf16(syn_cols),
    )


def dot(a, b):
    return jnp.dot(a, b, preferred_element_type=F32)


def lanes(shape):
    return lax.broadcasted_iota(jnp.int32, shape, len(shape) - 1)


def loop(count, body):
    def step(i, carry):
        body(i)
        return carry

    lax.fori_loop(0, count, step, 0)


def peer_at(me, k):
    dx, dy, core = FAR_FIRST[k]
    return ((me // 8 + dx) % 2) * 8 + (((me // 2) % 4 + dy) % 4) * 2 + (me + core) % 2


def at(i, width):
    return pl.ds(pl.multiple_of(i * width, width), width)


def kernel(
    image_hbm, dual_hbm, ids_ref, counts_ref, weights_hbm, data_hbm,
    tables_hbm, fourier_hbm, twiddle_hbm, ana_cols_hbm, ana_rows_hbm, syn_rows_hbm, syn_cols_hbm,
    image_out, dual_out,
    xpad, xwide, dual, weights, data, tables, fourier, twiddle, ana_cols, ana_rows, syn_rows, syn_cols,
    basis, folded, ysend, yrecv, hsend, hrecv, coeffs, trial, squares, near, far, quarter_sum, other_sum,
    factor, combined, edge_send, edge_recv, synth_wide, adjoint, wd_flat, wd_dense, forward, backward,
    packed, image_new, dual_new,
    local_sem, y_s, y_r, h_s, h_r, halo_s, halo_r, edge_s, edge_r, far_s, far_r, near_s, near_r,
    x_s, x_r, ga_s, ga_r, gb_s, gb_r, out_sem,
):
    me = lax.axis_index("strip")
    chan = lax.axis_index("chan")
    z = chan % 4
    x_hi = chan // 4
    zp, zm, zf = (z + 1) % 4, (z + 3) % 4, (z + 2) % 4
    up = {"chan": x_hi * 4 + zp}
    down = {"chan": x_hi * 4 + zm}
    across = {"chan": (1 - x_hi) * 4 + z}
    before, after = {"strip": (me + 15) % STRIPS}, {"strip": (me + 1) % STRIPS}
    sign = jnp.where(me < 8, 1, -1)

    loads = [
        pltpu.make_async_copy(src, dst, local_sem.at[i])
        for i, (src, dst) in enumerate(
            [
                (image_hbm, xpad.at[RIM : RIM + ROWS]),
                (tables_hbm, tables),
                (ana_cols_hbm, ana_cols),
                (ana_rows_hbm, ana_rows),
                (dual_hbm, dual),
                (weights_hbm, weights),
                (data_hbm, data),
                (fourier_hbm, fourier),
                (twiddle_hbm, twiddle),
                (syn_rows_hbm, syn_rows),
                (syn_cols_hbm, syn_cols),
            ]
        )
    ]
    for load in loads:
        load.start()

    barrier = pltpu.get_barrier_semaphore()
    for k in range(1, STRIPS):
        pl.semaphore_signal(
            barrier, inc=1, device_id={"strip": (me + k) % STRIPS}, device_id_type=MESH
        )
    for peer in (up, down, across):
        pl.semaphore_signal(barrier, inc=1, device_id=peer, device_id_type=MESH)
    pl.semaphore_wait(barrier, STRIPS + 2)

    def remote(src, dst, send, recv, peer):
        return pltpu.make_async_remote_copy(
            src_ref=src, dst_ref=dst, send_sem=send, recv_sem=recv, device_id=peer, device_id_type=MESH
        )

    halos = [
        remote(xpad.at[RIM : 2 * RIM], xpad.at[RIM + ROWS : PAD], halo_s.at[0], halo_r.at[0], before),
        remote(xpad.at[ROWS : RIM + ROWS], xpad.at[0:RIM], halo_s.at[1], halo_r.at[1], after),
    ]
    loads[0].wait()
    for copy in halos:
        copy.start()

    loads[1].wait()
    for parity in range(2):
        def make_basis(i, parity=parity):
            coarse_cos = tables[4 * parity, pl.ds(i, 1), :]
            coarse_sin = tables[4 * parity + 1, pl.ds(i, 1), :]
            block = coarse_cos * tables[4 * parity + 2] - coarse_sin * tables[4 * parity + 3]
            basis[parity, at(i, 32), :] = block.astype(BF16)

        loop(32, make_basis)
    left, right = xpad[RIM : RIM + ROWS, 0:1024], xpad[RIM : RIM + ROWS, 1024:2048]
    folded[0] = (left + right).astype(BF16)
    folded[1] = (left - right).astype(BF16)
    lane = lanes((ROWS, 128))
    edge_lane = (lane == 0) | (lane == 64)

    def y_copy(e, k):
        q = peer_at(me, k)
        return remote(ysend.at[e, q], yrecv.at[e, at(me, ROWS)], y_s.at[e, k], y_r.at[e, k], {"strip": q})

    for e in range(2):
        for pair in range(4):
            tiles = dot(folded[e], basis[e, :, 256 * pair : 256 * pair + 256])
            for half in range(2):
                tile = tiles[:, 128 * half : 128 * half + 128]
                p = 2 * pair + half
                ysend[e, p] = tile
                if e == 1:
                    ysend[e, 15 - p] = tile
        if e == 0:
            first = ysend[0, 0]
            for p in range(7):
                ysend[0, 15 - p] = jnp.where(edge_lane, ysend[0, p + 1], ysend[0, p])
            ysend[0, 8] = jnp.where(
                lane == 0, pltpu.roll(first, 64, 1), jnp.where(lane == 64, 0.0, ysend[0, 7])
            )
            ysend[0, 0] = jnp.where(lane == 64, 0.0, first)
        for k in range(15):
            y_copy(e, k).start()
        yrecv[e, at(me, ROWS), :] = ysend[e, me]

    for copy in halos:
        copy.wait_recv()
    for i in (2, 3, 4):
        loads[i].wait()
    xwide[:, 0:128] = jnp.zeros((PAD, 128), BF16)
    xwide[:, 128 + PIX : 256 + PIX] = jnp.zeros((PAD, 128), BF16)
    row = lax.broadcasted_iota(jnp.int32, (PAD, PIX), 0)
    outside = ((row < RIM) & (me == 0)) | ((row >= RIM + ROWS) & (me == STRIPS - 1))
    xwide[:, 128 : 128 + PIX] = jnp.where(outside, 0.0, xpad[...]).astype(BF16)

    def analyse_columns(i):
        for t in range(4):
            start = pl.multiple_of(i * 512 + t * 128, 128)
            both = dot(xwide[:, pl.ds(start, 384)], ana_cols[...]).astype(BF16)
            coeffs[0, :, pl.ds(start, 128)] = both[:, 0:128]
            coeffs[1, :, pl.ds(start, 128)] = both[:, 128:256]

    loop(4, analyse_columns)

    def far_copies(bank):
        return [
            remote(
                squares.at[bank, pl.ds(pl.multiple_of(zf * QUARTER, QUARTER), 16)],
                far.at[bank, 0], far_s.at[2 * bank], far_r.at[2 * bank], up,
            ),
            remote(
                squares.at[bank, pl.ds(pl.multiple_of(zf * QUARTER + 16, 16), 16)],
                far.at[bank, 1], far_s.at[2 * bank + 1], far_r.at[2 * bank + 1], down,
            ),
        ]

    def near_copies(bank):
        return [
            remote(
                squares.at[bank, at(zp, QUARTER)], near.at[bank, 0],
                near_s.at[2 * bank], near_r.at[2 * bank], up,
            ),
            remote(
                squares.at[bank, at(zm, QUARTER)], near.at[bank, 1],
                near_s.at[2 * bank + 1], near_r.at[2 * bank + 1], down,
            ),
        ]

    def x_copy(bank):
        return remote(quarter_sum.at[bank], other_sum.at[bank], x_s.at[bank], x_r.at[bank], across)

    def gather_near(bank):
        mine = factor.at[bank, at(z, QUARTER)]
        return [
            remote(mine, mine, ga_s.at[2 * bank], ga_r.at[2 * bank], up),
            remote(mine, mine, ga_s.at[2 * bank + 1], ga_r.at[2 * bank + 1], down),
        ]

    def gather_far(bank):
        low = factor.at[bank, pl.ds(pl.multiple_of(zm * QUARTER, QUARTER), 16)]
        high = factor.at[bank, pl.ds(pl.multiple_of(zp * QUARTER + 16, 16), 16)]
        return [
            remote(low, low, gb_s.at[2 * bank], gb_r.at[2 * bank], up),
            remote(high, high, gb_s.at[2 * bank + 1], gb_r.at[2 * bank + 1], down),
        ]

    for bank in range(BANKS):
        def analyse_rows(i, bank=bank):
            for t in range(4):
                cols = pl.ds(pl.multiple_of(i * 1024 + t * 256, 256), 256)
                values = dual[bank, :, cols].astype(F32) + dot(ana_rows[bank], coeffs[bank, :, cols])
                trial[bank, :, cols] = values
                squares[bank, :, cols] = values * values

        loop(2, analyse_rows)
        for copy in far_copies(bank):
            copy.start()

    for i in (5, 6, 7, 8):
        loads[i].wait()
    lane256 = lanes((128, 256))
    column = 2 * (lane256 % 64) + lane256 // 128
    column = jnp.where(me < 8, column, (128 - column) % 128)
    hit = lax.broadcasted_iota(jnp.int32, (128, 256), 0) == column
    imag_lane = (lane256 // 64) % 2 == 1
    pick_both = jnp.where(hit, 1.0, 0.0).astype(BF16)
    pick_real = jnp.where(hit & ~imag_lane, 1.0, 0.0).astype(BF16)
    pick_imag = (jnp.where(hit & imag_lane, 1.0, 0.0) * sign.astype(F32)).astype(BF16)

    def pick_columns(i):
        rows = at(i, 256)
        blocks = at(i, 8)
        flat = (
            dot(weights[blocks].reshape(256, 128), pick_both),
            dot(data[0, blocks].reshape(256, 128), pick_real)
            + dot(data[1, blocks].reshape(256, 128), pick_imag),
        )
        for kind in range(2):
            for half in range(2):
                wd_flat[2 * kind + half, rows, :] = flat[kind][:, 128 * half : 128 * half + 128]

    loop(4, pick_columns)
    slot = lanes((8, 32))
    ids = jnp.broadcast_to(ids_ref[...], (8, 32))
    live_ids = jnp.where(slot < counts_ref[...], ids, -1).astype(F32).astype(BF16)
    spread = jnp.where(
        lanes((32, 256)) // 8 == lax.broadcasted_iota(jnp.int32, (32, 256), 0), 1.0, 0.0
    ).astype(BF16)
    slot_ids = dot(live_ids, spread)[0:1, :].astype(jnp.int32)
    place_row = lax.broadcasted_iota(jnp.int32, (512, 256), 0)
    place_col = lanes((512, 256))
    place = jnp.where(
        (slot_ids == place_row // 8) & (place_row % 8 == place_col % 8), 1.0, 0.0
    ).astype(BF16)
    for kind in range(2):
        for u in range(4):
            picked = jnp.concatenate(
                [
                    wd_flat[2 * kind, pl.ds(u, 256, stride=4), :],
                    wd_flat[2 * kind + 1, pl.ds(u, 256, stride=4), :],
                ],
                axis=1,
            ).astype(BF16)
            spread_out = dot(place, picked).astype(BF16)
            wd_dense[kind, 0, u] = spread_out[:, 0:128]
            wd_dense[kind, 1, u] = spread_out[:, 128:256]

    for bank in range(BANKS):
        for copy in far_copies(bank):
            copy.wait_recv()
        low = pl.ds(pl.multiple_of(zp * QUARTER, QUARTER), 16)
        high = pl.ds(pl.multiple_of(zm * QUARTER + 16, 16), 16)
        squares[bank, low, :] = squares[bank, low, :] + far[bank, 0]
        squares[bank, high, :] = squares[bank, high, :] + far[bank, 1]
        for copy in near_copies(bank):
            copy.start()
    for bank in range(BANKS):
        for copy in near_copies(bank):
            copy.wait_recv()
        quarter_sum[bank] = squares[bank, at(z, QUARTER), :] + near[bank, 0] + near[bank, 1]
        x_copy(bank).start()

    lane_sign = jnp.where(lanes((1, 128)) < 64, -sign, sign).astype(F32)

    def times_i(values):
        return lane_sign * pltpu.roll(values, 64, 1)

    def h_copy(e, k):
        q = peer_at(me, k)
        return remote(hsend.at[e, at(q, ROWS)], hrecv.at[e, me], h_s.at[e, k], h_r.at[e, k], {"strip": q})

    def column_stage(e):
        for k in range(15):
            y_copy(e, k).wait_recv()

        def fold_rows(i):
            for part in range(2):
                start = i * 128 + part * 64
                rows = pl.ds(pl.multiple_of(start, 64), 64)
                low = pl.ds(pl.multiple_of(512 + start, 64), 64)
                y0, y1, y2, y3 = (
                    yrecv[e, pl.ds(pl.multiple_of(512 * j + start, 64), 64), :] for j in range(4)
                )
                tw = twiddle[rows, :]
                sum_a, sum_b, dif_a, dif_b = y0 + y2, y1 + y3, y0 - y2, y1 - y3
                total, alt = sum_a + sum_b, sum_a - sum_b
                turned_a, turned_b = times_i(dif_a), times_i(dif_b)
                folds = (
                    (total, times_i(total)),
                    (dif_a - turned_b, turned_a + dif_b),
                    (alt, times_i(alt)),
                    (dif_a + turned_b, turned_a - dif_b),
                )
                for u, (value, turned) in enumerate(folds):
                    if u > 0:
                        cos, sin = tw[:, 2 * u - 2 : 2 * u - 1], tw[:, 2 * u - 1 : 2 * u]
                        value, turned = cos * value - sin * turned, cos * turned + sin * value
                    lanes_of = slice(128 * (u % 2), 128 * (u % 2) + 128)
                    forward[u // 2, rows, lanes_of] = value.astype(BF16)
                    forward[u // 2, low, lanes_of] = (-turned).astype(BF16)

        loop(4, fold_rows)
        for pair in range(2):
            for m in range(2):
                rows, low = slice(256 * m, 256 * m + 256), slice(512 + 256 * m, 768 + 256 * m)
                both = dot(fourier[rows, :], forward[pair])
                for half in range(2):
                    u = 2 * pair + half
                    spectrum = both[:, 128 * half : 128 * half + 128]
                    weight = wd_dense[0, e, u, rows, :].astype(F32)
                    residual = weight * (weight * spectrum - wd_dense[1, e, u, rows, :].astype(F32))
                    turned = times_i(residual).astype(BF16)
                    residual = residual.astype(BF16)
                    backward[u, rows, 0:128] = residual
                    backward[u, low, 0:128] = turned
                    if u > 0:
                        backward[u, rows, 128:256] = turned
                        backward[u, low, 128:256] = -residual
        for m in range(4):
            rows = slice(128 * m, 128 * m + 128)
            left_side = fourier[rows, :]
            tw = twiddle[rows, :]
            terms = [dot(left_side, backward[0, :, 0:128])]
            for u in (1, 2, 3):
                both = dot(left_side, backward[u])
                cos, sin = tw[:, 2 * u - 2 : 2 * u - 1], tw[:, 2 * u - 1 : 2 * u]
                value, turned = both[:, 0:128], both[:, 128:256]
                terms.append(cos * value + sin * turned)
                if u == 1:
                    turned_odd = cos * turned - sin * value
                if u == 3:
                    turned_odd = turned_odd - (cos * turned - sin * value)
            plus, minus, odd = terms[0] + terms[2], terms[0] - terms[2], terms[1] + terms[3]
            for j, value in enumerate((plus + odd, minus + turned_odd, plus - odd, minus - turned_odd)):
                hsend[e, 512 * j + 128 * m : 512 * j + 128 * m + 128, :] = value
        for k in range(15):
            h_copy(e, k).start()
        hrecv[e, me] = hsend[e, at(me, ROWS), :]

    column_stage(0)
    bound = shrink_level * math.sqrt(8.0)
    for bank in range(BANKS):
        x_copy(bank).wait_recv()
        total = quarter_sum[bank] + other_sum[bank]
        factor[bank, at(z, QUARTER), :] = bound / jnp.maximum(jnp.sqrt(total), bound)
        for copy in gather_near(bank):
            copy.start()
    column_stage(1)
    for bank in range(BANKS):
        for copy in gather_near(bank):
            copy.wait_recv()
        for copy in gather_far(bank):
            copy.start()

    dual_outs = []
    for bank in range(BANKS):
        for copy in gather_far(bank):
            copy.wait_recv()

        def shrink(i, bank=bank):
            rows = at(i, 16)
            fresh = (trial[bank, rows, :] * factor[bank, rows, :]).astype(BF16)
            dual_new[bank, rows, :] = fresh
            inner = pl.ds(pl.multiple_of(RIM + i * 16, 8), 16)
            combined[bank, inner, :] = 2.0 * fresh.astype(F32) - dual[bank, rows, :].astype(F32)

        loop(8, shrink)
        edge_send[bank, 0] = combined[bank, RIM : 2 * RIM]
        edge_send[bank, 1] = combined[bank, ROWS : RIM + ROWS]
        for copy in edge_copies(remote, bank, edge_send, edge_recv, edge_s, edge_r, before, after):
            copy.start()
    dual_copy = pltpu.make_async_copy(dual_new, dual_out, out_sem.at[0])
    dual_copy.start()

    for bank in range(BANKS):
        for copy in edge_copies(remote, bank, edge_send, edge_recv, edge_s, edge_r, before, after):
            copy.wait_recv()
        combined[bank, RIM + ROWS : PAD] = jnp.where(me == STRIPS - 1, 0.0, edge_recv[bank, 0])
        combined[bank, 0:RIM] = jnp.where(me == 0, 0.0, edge_recv[bank, 1])
    for i in (9, 10):
        loads[i].wait()
    for bank in range(BANKS):
        synth_wide[bank, :, 0:128] = jnp.zeros((ROWS, 128), BF16)
        synth_wide[bank, :, 128 + PIX : 256 + PIX] = jnp.zeros((ROWS, 128), BF16)

        def synthesise_rows(i, bank=bank):
            for t in range(4):
                start = i * 1024 + t * 256
                cols = pl.ds(pl.multiple_of(start, 256), 256)
                values = dot(syn_rows[bank], combined[bank, :, cols].astype(BF16))
                synth_wide[bank, :, pl.ds(pl.multiple_of(128 + start, 128), 256)] = values.astype(BF16)

        loop(2, synthesise_rows)

    def synthesise_columns(i):
        for t in range(4):
            start = pl.multiple_of(i * 512 + t * 128, 128)
            window = pl.ds(start, 384)
            adjoint[:, pl.ds(start, 128)] = dot(synth_wide[0, :, window], syn_cols[0:384]) + dot(
                synth_wide[1, :, window], syn_cols[384:768]
            )

    loop(4, synthesise_columns)

    for e in range(2):
        for k in range(15):
            h_copy(e, k).wait_recv()
        for p in range(8):
            value = hrecv[e, p]
            if e == 1:
                value = value + hrecv[e, 15 - p]
            elif p == 0:
                value = jnp.where(
                    lane == 0, value,
                    jnp.where(lane == 64, pltpu.roll(hrecv[0, 8], 64, 1), value + hrecv[0, 15]),
                )
            else:
                value = value + jnp.where(edge_lane, hrecv[0, 16 - p], hrecv[0, 15 - p])
            packed[e, :, 128 * p : 128 * p + 128] = value.astype(BF16)

    def finish(i):
        cols = at(i, 256)
        turn = (((1,), (1,)), ((), ()))
        even, odd = (
            lax.dot_general(packed[j], basis[j, cols, :], turn, preferred_element_type=F32)
            for j in range(2)
        )
        for gradient, where in (
            (even + odd, cols),
            (even - odd, pl.ds(pl.multiple_of(1024 + i * 256, 256), 256)),
        ):
            image_new[:, where] = jnp.maximum(
                xpad[RIM : RIM + ROWS, where] - tau_primal * (gradient + adjoint[:, where]), 0.0
            )

    loop(4, finish)
    image_copy = pltpu.make_async_copy(image_new, image_out, out_sem.at[1])
    image_copy.start()

    for copy in halos:
        copy.wait_send()
    for e in range(2):
        for k in range(15):
            y_copy(e, k).wait_send()
            h_copy(e, k).wait_send()
    for bank in range(BANKS):
        for copy in far_copies(bank) + near_copies(bank) + gather_near(bank) + gather_far(bank):
            copy.wait_send()
        x_copy(bank).wait_send()
        for copy in edge_copies(remote, bank, edge_send, edge_recv, edge_s, edge_r, before, after):
            copy.wait_send()
    dual_copy.wait()
    image_copy.wait()


def edge_copies(remote, bank, edge_send, edge_recv, edge_s, edge_r, before, after):
    return [
        remote(
            edge_send.at[bank, side], edge_recv.at[bank, side],
            edge_s.at[2 * bank + side], edge_r.at[2 * bank + side], (before, after)[side],
        )
        for side in range(2)
    ]


def per_device(constants, image, dual_coeffs, block_ids, block_counts, block_weights, block_data):
    any_space = pl.BlockSpec(memory_space=pl.ANY)
    in_vmem = pl.BlockSpec(memory_space=pltpu.VMEM)
    dma = lambda *n: pltpu.SemaphoreType.DMA(n)
    vmem = pltpu.VMEM
    image_new, dual_new = pl.pallas_call(
        kernel,
        out_shape=(
            jax.ShapeDtypeStruct((ROWS, PIX), F32),
            jax.ShapeDtypeStruct((BANKS, ROWS, PIX), BF16),
        ),
        in_specs=[any_space, any_space, in_vmem, in_vmem] + [any_space] * 9,
        out_specs=(any_space, any_space),
        scratch_shapes=[
            vmem((PAD, PIX), F32),
            vmem((PAD, PIX + 256), BF16),
            vmem((BANKS, ROWS, PIX), BF16),
            vmem((32, 32, 128), BF16),
            vmem((2, 32, 32, 128), BF16),
            vmem((8, 32, 1024), F32),
            vmem((512, 1024), BF16),
            vmem((512, 128), F32),
            vmem((384, 256), BF16),
            vmem((BANKS, ROWS, PAD), BF16),
            vmem((BANKS, ROWS, PAD), BF16),
            vmem((768, 128), BF16),
            vmem((2, 1024, 1024), BF16),
            vmem((2, ROWS, 1024), BF16),
            vmem((2, STRIPS, ROWS, 128), F32),
            vmem((2, PIX, 128), F32),
            vmem((2, PIX, 128), F32),
            vmem((2, STRIPS, ROWS, 128), F32),
            vmem((BANKS, PAD, PIX), BF16),
            vmem((BANKS, ROWS, PIX), F32),
            vmem((BANKS, ROWS, PIX), F32),
            vmem((BANKS, 2, QUARTER, PIX), F32),
            vmem((BANKS, 2, 16, PIX), F32),
            vmem((BANKS, QUARTER, PIX), F32),
            vmem((BANKS, QUARTER, PIX), F32),
            vmem((BANKS, ROWS, PIX), F32),
            vmem((BANKS, PAD, PIX), F32),
            vmem((BANKS, 2, RIM, PIX), F32),
            vmem((BANKS, 2, RIM, PIX), F32),
            vmem((BANKS, ROWS, PIX + 256), BF16),
            vmem((ROWS, PIX), F32),
            vmem((4, 1024, 128), F32),
            vmem((2, 2, 4, 512, 128), BF16),
            vmem((2, 1024, 256), BF16),
            vmem((4, 1024, 256), BF16),
            vmem((2, ROWS, 1024), BF16),
            vmem((ROWS, PIX), F32),
            vmem((BANKS, ROWS, PIX), BF16),
            dma(11), dma(2, 15), dma(2, 15), dma(2, 15), dma(2, 15), dma(2), dma(2), dma(4), dma(4),
            dma(4), dma(4), dma(4), dma(4), dma(2), dma(2), dma(4), dma(4), dma(4), dma(4), dma(2),
        ],
        compiler_params=pltpu.CompilerParams(
            collective_id=0, has_side_effects=True, vmem_limit_bytes=60 * 1024 * 1024
        ),
    )(
        image[0],
        dual_coeffs[:, 0],
        block_ids,
        block_counts,
        block_weights[0],
        block_data[0],
        *constants,
    )
    return image_new[None], dual_new[:, None]


def solution(mesh):
    constants = tuple(jnp.asarray(c) for c in make_constants())

    def body(*args):
        return per_device(constants, *args)

    return jax.shard_map(
        body,
        mesh=mesh,
        in_specs=(
            P("chan", "strip", None),
            P(None, "chan", "strip", None),
            P("chan", "strip"),
            P("chan", "strip"),
            P("chan", "strip", None, None),
            P("chan", None, "strip", None, None),
        ),
        out_specs=(P("chan", "strip", None), P(None, "chan", "strip", None)),
        check_vma=False,
    )
```

```python
import math

import jax
import jax.numpy as jnp
import numpy as np
from jax import lax
from jax.experimental import pallas as pl
from jax.experimental.pallas import tpu as pltpu
from jax.sharding import PartitionSpec as P

MESH = pl.DeviceIdType.MESH
F32, BF16 = jnp.float32, jnp.bfloat16

PIX = 2048
ROWS = 128
STRIPS = 16
RIM = 8
PAD = ROWS + 2 * RIM
BANKS = 2
QUARTER = ROWS // 4
FAR_FIRST = [
    (dx, dy, core)
    for dx, dy in ((1, 2), (0, 2), (1, 1), (1, 3), (0, 1), (0, 3), (1, 0))
    for core in (0, 1)
] + [(0, 0, 1)]

root_three = math.sqrt(3.0)
sqrt_two = math.sqrt(2.0)
daub_two = [
    (1.0 + root_three) / (4.0 * sqrt_two),
    (3.0 + root_three) / (4.0 * sqrt_two),
    (3.0 - root_three) / (4.0 * sqrt_two),
    (1.0 - root_three) / (4.0 * sqrt_two),
]
daub_four = [
    0.2303778133088964,
    0.7148465705529155,
    0.6308807679298587,
    -0.0279837694168599,
    -0.1870348117190931,
    0.0308413818355607,
    0.0328830116668852,
    -0.010597401785069,
]
bank_filters = [daub_two, daub_four]
sigma_dual = 0.5
tau_primal = 0.3
shrink_level = 0.5


def bank_matrix(taps, out_at, out_count, in_at, in_count):
    count = len(taps)
    high = [(-1) ** k * taps[count - 1 - k] for k in range(count)]
    offset = count // 2 - 1
    matrix = np.zeros((out_count, in_count), np.float64)
    for i in range(out_count):
        m = out_at + i
        even = m - m % 2
        for k in range(count):
            n = even + k - offset - in_at
            if 0 <= n < in_count:
                matrix[i, n] = (taps if m % 2 == 0 else high)[k]
    return matrix


def make_constants():
    two_pi = 2.0 * math.pi
    tables = []
    for parity in range(2):
        tile, part, k = np.meshgrid(np.arange(8), np.arange(2), np.arange(64), indexing="ij")
        freq = 128 * tile + 2 * k + parity
        phase = part * (math.pi / 2)
        if parity == 0:
            freq[0, 1, 0] = PIX // 2
            phase = phase.copy()
            phase[0, 1, 0] = 0.0
        freq, phase = freq.reshape(-1), phase.reshape(-1)
        coarse = two_pi * (32 * np.arange(32)[:, None] * freq[None, :] % PIX) / PIX
        fine = two_pi * (np.arange(32)[:, None] * freq[None, :] % PIX) / PIX + phase[None, :]
        tables += [np.cos(coarse), np.sin(coarse), np.cos(fine) / 32.0, np.sin(fine) / 32.0]
    tables = np.stack(tables).astype(np.float32)
    grid = two_pi * (np.arange(512)[:, None] * np.arange(512)[None, :] % 512) / 512
    fourier = np.concatenate([np.cos(grid), np.sin(grid)], axis=1) / 64.0
    twiddle = np.zeros((512, 128), np.float32)
    for u in (1, 2, 3):
        angle = two_pi * (np.arange(512) * u) / PIX
        twiddle[:, 2 * u - 2] = np.cos(angle)
        twiddle[:, 2 * u - 1] = np.sin(angle)
    ana_cols = np.concatenate(
        [bank_matrix(t, 128, 128, 0, 384).T for t in bank_filters], axis=1
    )
    ana_rows = np.stack([sigma_dual * bank_matrix(t, RIM, ROWS, 0, PAD) for t in bank_filters])
    syn_rows = np.stack([bank_matrix(t, 0, PAD, RIM, ROWS).T for t in bank_filters])
    syn_cols = np.concatenate([bank_matrix(t, 0, 384, 128, 128) for t in bank_filters], axis=0)
    as_bf16 = lambda a: np.asarray(a, np.float32).astype(BF16)
    return (
        tables,
        as_bf16(fourier),
        twiddle,
        as_bf16(ana_cols),
        as_bf16(ana_rows),
        as_bf16(syn_rows),
        as_bf16(syn_cols),
    )


def dot(a, b):
    return jnp.dot(a, b, preferred_element_type=F32)


def lanes(shape):
    return lax.broadcasted_iota(jnp.int32, shape, len(shape) - 1)


def loop(count, body):
    def step(i, carry):
        body(i)
        return carry

    lax.fori_loop(0, count, step, 0)


def peer_at(me, k):
    dx, dy, core = FAR_FIRST[k]
    return ((me // 8 + dx) % 2) * 8 + (((me // 2) % 4 + dy) % 4) * 2 + (me + core) % 2


def at(i, width):
    return pl.ds(pl.multiple_of(i * width, width), width)


def kernel(
    image_hbm, dual_hbm, ids_ref, counts_ref, weights_hbm, data_hbm,
    tables_hbm, fourier_hbm, twiddle_hbm, ana_cols_hbm, ana_rows_hbm, syn_rows_hbm, syn_cols_hbm,
    image_out, dual_out,
    xpad, xwide, dual, weights, data, tables, fourier, twiddle, ana_cols, ana_rows, syn_rows, syn_cols,
    basis, folded, ysend, yrecv, hsend, hrecv, coeffs, trial, squares, near, far, quarter_sum, other_sum,
    factor, combined, edge_send, edge_recv, synth_wide, adjoint, own_flat, other_flat, rim_flat,
    w_send, w_recv, d_send, d_recv, ids_send, ids_recv, rim_send, rim_recv, wd_dense,
    forward, kept, backward, packed, image_new, dual_new,
    local_sem, y_s, y_r, h_s, h_r, halo_s, halo_r, edge_s, edge_r, far_s, far_r, near_s, near_r,
    x_s, x_r, ga_s, ga_r, gb_s, gb_r, swap_s, swap_r, out_sem,
):
    me = lax.axis_index("strip")
    chan = lax.axis_index("chan")
    z = chan % 4
    x_hi = chan // 4
    zp, zm, zf = (z + 1) % 4, (z + 3) % 4, (z + 2) % 4
    up = {"chan": x_hi * 4 + zp}
    down = {"chan": x_hi * 4 + zm}
    across = {"chan": (1 - x_hi) * 4 + z}
    before, after = {"strip": (me + 15) % STRIPS}, {"strip": (me + 1) % STRIPS}
    sign = jnp.where(me < 8, 1, -1)

    loads = [
        pltpu.make_async_copy(src, dst, local_sem.at[i])
        for i, (src, dst) in enumerate(
            [
                (tables_hbm, tables),
                (image_hbm, xpad.at[RIM : RIM + ROWS]),
                (ana_cols_hbm, ana_cols),
                (ana_rows_hbm, ana_rows),
                (dual_hbm, dual),
                (weights_hbm, weights),
                (data_hbm, data),
                (fourier_hbm, fourier),
                (twiddle_hbm, twiddle),
                (syn_rows_hbm, syn_rows),
                (syn_cols_hbm, syn_cols),
            ]
        )
    ]
    for load in loads:
        load.start()

    barrier = pltpu.get_barrier_semaphore()
    for k in range(1, STRIPS):
        pl.semaphore_signal(
            barrier, inc=1, device_id={"strip": (me + k) % STRIPS}, device_id_type=MESH
        )
    for peer in (up, down, across):
        pl.semaphore_signal(barrier, inc=1, device_id=peer, device_id_type=MESH)
    pl.semaphore_wait(barrier, STRIPS + 2)

    def remote(src, dst, send, recv, peer):
        return pltpu.make_async_remote_copy(
            src_ref=src, dst_ref=dst, send_sem=send, recv_sem=recv, device_id=peer, device_id_type=MESH
        )

    halos = [
        remote(xpad.at[RIM : 2 * RIM], xpad.at[RIM + ROWS : PAD], halo_s.at[0], halo_r.at[0], before),
        remote(xpad.at[ROWS : RIM + ROWS], xpad.at[0:RIM], halo_s.at[1], halo_r.at[1], after),
    ]
    loads[0].wait()
    for parity in range(2):
        def make_basis(i, parity=parity):
            coarse_cos = tables[4 * parity, pl.ds(i, 1), :]
            coarse_sin = tables[4 * parity + 1, pl.ds(i, 1), :]
            block = coarse_cos * tables[4 * parity + 2] - coarse_sin * tables[4 * parity + 3]
            basis[parity, at(i, 32), :] = block.astype(BF16)

        loop(32, make_basis)
    loads[1].wait()
    for copy in halos:
        copy.start()
    left, right = xpad[RIM : RIM + ROWS, 0:1024], xpad[RIM : RIM + ROWS, 1024:2048]
    folded[0] = (left + right).astype(BF16)
    folded[1] = (left - right).astype(BF16)
    def y_copy(k):
        q = peer_at(me, k)
        return remote(ysend.at[q], yrecv.at[at(me, ROWS)], y_s.at[k], y_r.at[k], {"strip": q})

    for e in range(2):
        for pair in range(4):
            tiles = dot(folded[e], basis[e, :, 256 * pair : 256 * pair + 256])
            for half in range(2):
                p = 2 * pair + half
                ysend[15 - p if e else p] = tiles[:, 128 * half : 128 * half + 128]
    for k in range(15):
        y_copy(k).start()
    yrecv[at(me, ROWS), :] = ysend[me]

    for copy in halos:
        copy.wait_recv()
    for i in (2, 3, 4):
        loads[i].wait()
    xwide[:, 0:128] = jnp.zeros((PAD, 128), BF16)
    xwide[:, 128 + PIX : 256 + PIX] = jnp.zeros((PAD, 128), BF16)
    row = lax.broadcasted_iota(jnp.int32, (PAD, PIX), 0)
    outside = ((row < RIM) & (me == 0)) | ((row >= RIM + ROWS) & (me == STRIPS - 1))
    xwide[:, 128 : 128 + PIX] = jnp.where(outside, 0.0, xpad[...]).astype(BF16)

    def analyse_columns(i):
        for t in range(4):
            start = pl.multiple_of(i * 512 + t * 128, 128)
            both = dot(xwide[:, pl.ds(start, 384)], ana_cols[...]).astype(BF16)
            coeffs[0, :, pl.ds(start, 128)] = both[:, 0:128]
            coeffs[1, :, pl.ds(start, 128)] = both[:, 128:256]

    loop(4, analyse_columns)

    def far_copies(bank):
        return [
            remote(
                squares.at[bank, pl.ds(pl.multiple_of(zf * QUARTER, QUARTER), 16)],
                far.at[bank, 0], far_s.at[2 * bank], far_r.at[2 * bank], up,
            ),
            remote(
                squares.at[bank, pl.ds(pl.multiple_of(zf * QUARTER + 16, 16), 16)],
                far.at[bank, 1], far_s.at[2 * bank + 1], far_r.at[2 * bank + 1], down,
            ),
        ]

    def near_copies(bank):
        return [
            remote(
                squares.at[bank, at(zp, QUARTER)], near.at[bank, 0],
                near_s.at[2 * bank], near_r.at[2 * bank], up,
            ),
            remote(
                squares.at[bank, at(zm, QUARTER)], near.at[bank, 1],
                near_s.at[2 * bank + 1], near_r.at[2 * bank + 1], down,
            ),
        ]

    def x_copy(bank):
        return remote(quarter_sum.at[bank], other_sum.at[bank], x_s.at[bank], x_r.at[bank], across)

    def gather_near(bank):
        mine = factor.at[bank, at(z, QUARTER)]
        return [
            remote(mine, mine, ga_s.at[2 * bank], ga_r.at[2 * bank], up),
            remote(mine, mine, ga_s.at[2 * bank + 1], ga_r.at[2 * bank + 1], down),
        ]

    def gather_far(bank):
        low = factor.at[bank, pl.ds(pl.multiple_of(zm * QUARTER, QUARTER), 16)]
        high = factor.at[bank, pl.ds(pl.multiple_of(zp * QUARTER + 16, 16), 16)]
        return [
            remote(low, low, gb_s.at[2 * bank], gb_r.at[2 * bank], up),
            remote(high, high, gb_s.at[2 * bank + 1], gb_r.at[2 * bank + 1], down),
        ]

    for bank in range(BANKS):
        def analyse_rows(i, bank=bank):
            for t in range(4):
                cols = pl.ds(pl.multiple_of(i * 1024 + t * 256, 256), 256)
                values = dual[bank, :, cols].astype(F32) + dot(ana_rows[bank], coeffs[bank, :, cols])
                trial[bank, :, cols] = values
                squares[bank, :, cols] = values * values

        loop(2, analyse_rows)
        for copy in far_copies(bank):
            copy.start()

    for i in (5, 6, 7, 8):
        loads[i].wait()
    lane_of = lanes((128, 128))
    half_lane = lane_of % 64
    imag_lane = lane_of >= 64
    column_row = lax.broadcasted_iota(jnp.int32, (128, 128), 0)
    own_hit = column_row == jnp.where(me < 8, 2 * half_lane, 127 - 2 * half_lane)
    other_hit = column_row == jnp.where(me < 8, 2 * half_lane + 1, 128 - 2 * half_lane)
    one_hot = lambda mask: jnp.where(mask, 1.0, 0.0).astype(BF16)
    signed = lambda mask: jnp.where(mask, sign.astype(F32), 0.0).astype(BF16)
    own_real, own_imag = one_hot(own_hit & ~imag_lane), signed(own_hit & imag_lane)
    other_real, other_imag = one_hot(other_hit & ~imag_lane), signed(other_hit & imag_lane)
    other_low, other_high = one_hot(other_hit & ~imag_lane), one_hot(other_hit & imag_lane)
    mirror = {"strip": 15 - me}
    rim_peer = {"strip": jnp.where(me < 8, 8 + (8 - me) % 8, (16 - me) % 8)}

    def picked_rows(ref, i):
        return ref[8 * i : 8 * i + 8].reshape(256, 128)

    for i in range(4):
        rows = slice(256 * i, 256 * i + 256)
        d_send[rows, :] = dot(picked_rows(data.at[0], i), other_real) + dot(
            picked_rows(data.at[1], i), other_imag
        )
        if i < 2:
            w_send[rows, :] = dot(picked_rows(weights, i), other_low) + dot(
                picked_rows(weights, i + 2), other_high
            )
    slot = lanes((8, 32))
    ids = jnp.broadcast_to(ids_ref[...], (8, 32))
    live_ids = jnp.where(slot < counts_ref[...], ids, -1).astype(F32).astype(BF16)
    spread = jnp.where(
        lanes((32, 256)) // 8 == lax.broadcasted_iota(jnp.int32, (32, 256), 0), 1.0, 0.0
    ).astype(BF16)
    ids_send[...] = dot(live_ids, spread)
    sel_row, sel_lane = lax.broadcasted_iota(jnp.int32, (8, 128), 0), lanes((8, 128))
    turn = (((1,), (1,)), ((), ()))
    rim = 0.0
    for i, values in enumerate((weights[...], data[0], data[1])):
        select = one_hot((sel_row == i) & (sel_lane == 0))
        rim = rim + lax.dot_general(select, values.reshape(1024, 128), turn, preferred_element_type=F32)
    rim_send[...] = rim
    swaps = [
        remote(w_send, w_recv, swap_s.at[0], swap_r.at[0], mirror),
        remote(ids_send, ids_recv.at[0], swap_s.at[1], swap_r.at[1], mirror),
        remote(ids_send, ids_recv.at[1], swap_s.at[2], swap_r.at[2], rim_peer),
        remote(rim_send, rim_recv, swap_s.at[3], swap_r.at[3], rim_peer),
        remote(d_send.at[0:512], d_recv.at[0:512], swap_s.at[4], swap_r.at[4], mirror),
        remote(d_send.at[512:1024], d_recv.at[512:1024], swap_s.at[5], swap_r.at[5], mirror),
    ]
    for copy in swaps[0:5]:
        copy.start()

    for i in range(4):
        rows = slice(256 * i, 256 * i + 256)
        own_flat[0, rows, :] = dot(picked_rows(weights, i), one_hot(own_hit))
        own_flat[1, rows, :] = dot(picked_rows(data.at[0], i), own_real) + dot(
            picked_rows(data.at[1], i), own_imag
        )
    place_row = lax.broadcasted_iota(jnp.int32, (512, 256), 0)
    same_row = place_row % 8 == lanes((512, 256)) % 8

    def place_of(slot_ids):
        return one_hot((slot_ids[0:1, :].astype(jnp.int32) == place_row // 8) & same_row)

    def by_row(flat_w, flat_d, u):
        rows = pl.ds(u, 256, stride=4)
        return jnp.concatenate([flat_w[rows, :], flat_d[rows, :]], axis=1).astype(BF16)

    def put_dense(role, u, values):
        values = values.astype(BF16)
        wd_dense[role, 0, u] = values[:, 0:128]
        wd_dense[role, 1, u] = values[:, 128:256]

    own_place = place_of(ids_send[...])
    for u in range(4):
        put_dense(0, u, dot(own_place, by_row(own_flat.at[0], own_flat.at[1], u)))

    lane_sign = jnp.where(lanes((1, 128)) < 64, -sign, sign).astype(F32)
    swap_halves = lambda values: pltpu.roll(values, 64, 1)
    first_lane = (lanes((1, 128)) == 0) & (me == 0)
    middle_lane = (lanes((1, 128)) == 64) & (me == 0)

    def times_i(values):
        return lane_sign * swap_halves(values)

    def h_copy(k):
        q = peer_at(me, k)
        return remote(hsend.at[at(q, ROWS)], hrecv.at[me], h_s.at[k], h_r.at[k], {"strip": q})

    def fold_rows(i):
        for part in range(2):
            start = i * 128 + part * 64
            rows = pl.ds(pl.multiple_of(start, 64), 64)
            low = pl.ds(pl.multiple_of(512 + start, 64), 64)
            loaded = [yrecv[pl.ds(pl.multiple_of(512 * j + start, 64), 64), :] for j in range(4)]
            tw = twiddle[rows, :]
            for role in range(2):
                if role == 0:
                    parts = [jnp.where(middle_lane, 0.0, y) for y in loaded]
                else:
                    parts = [
                        jnp.where(first_lane, swap_halves(y), jnp.where(middle_lane, 0.0, y)) for y in loaded
                    ]
                unit = times_i if role == 0 else (lambda values: -times_i(values))
                y0, y1, y2, y3 = parts
                sum_a, sum_b, dif_a, dif_b = y0 + y2, y1 + y3, y0 - y2, y1 - y3
                total, alt = sum_a + sum_b, sum_a - sum_b
                turned_a, turned_b = unit(dif_a), unit(dif_b)
                folds = (
                    (total, unit(total)),
                    (dif_a - turned_b, turned_a + dif_b),
                    (alt, unit(alt)),
                    (dif_a + turned_b, turned_a - dif_b),
                )
                lanes_of = slice(128 * role, 128 * role + 128)
                for u, (value, turned) in enumerate(folds):
                    if u > 0:
                        cos, sin = tw[:, 2 * u - 2 : 2 * u - 1], tw[:, 2 * u - 1 : 2 * u]
                        value, turned = cos * value - sin * turned, cos * turned + sin * value
                    forward[u, rows, lanes_of] = value.astype(BF16)
                    forward[u, low, lanes_of] = (-turned).astype(BF16)

    def weigh(role, u, rows, spectrum):
        weight = wd_dense[role, 0, u, rows, :].astype(F32)
        return weight * (weight * spectrum - wd_dense[role, 1, u, rows, :].astype(F32))

    def transform_columns():
        for k in range(15):
            y_copy(k).wait_recv()
        loop(4, fold_rows)
        for u in range(4):
            for m in range(2):
                rows = slice(256 * m, 256 * m + 256)
                both = dot(fourier[rows, :], forward[u])
                kept[0, u, rows, :] = weigh(0, u, rows, both[:, 0:128])
                kept[1, u, rows, :] = both[:, 128:256]

    def receive_swaps():
        for copy in swaps:
            copy.wait_recv()
        for m in range(2):
            rows = slice(256 * m, 256 * m + 256)
            values = w_recv[rows, :]
            turned = swap_halves(values)
            left_lane = lanes((256, 128)) < 64
            other_flat[256 * m : 256 * m + 256, :] = jnp.where(left_lane, values, turned)
            other_flat[512 + 256 * m : 768 + 256 * m, :] = jnp.where(left_lane, turned, values)
        rims = jnp.concatenate([rim_recv[...], jnp.zeros((120, 1024), F32)], axis=0).T.astype(BF16)
        has_rim = me < 8
        rim_w = one_hot((column_row == 0) & (half_lane == 0) & has_rim)
        rim_d = one_hot((column_row == 1) & (lane_of == 0) & has_rim) - one_hot(
            (column_row == 2) & (lane_of == 64) & has_rim
        )
        rim_flat[0] = dot(rims, rim_w)
        rim_flat[1] = dot(rims, rim_d)
        other_place, rim_place = place_of(ids_recv[0]), place_of(ids_recv[1])
        for u in range(4):
            put_dense(
                1, u,
                dot(other_place, by_row(other_flat, d_recv, u))
                + dot(rim_place, by_row(rim_flat.at[0], rim_flat.at[1], u)),
            )

    def transform_back():
        for u in range(4):
            for m in range(2):
                rows, low = slice(256 * m, 256 * m + 256), slice(512 + 256 * m, 768 + 256 * m)
                own, other = kept[0, u, rows, :], weigh(1, u, rows, kept[1, u, rows, :])
                own_turned, other_swapped = times_i(own), swap_halves(other)
                value = jnp.where(first_lane, own, jnp.where(middle_lane, other_swapped, own + other))
                turned = jnp.where(
                    first_lane, own_turned,
                    jnp.where(middle_lane, other, own_turned - lane_sign * other_swapped),
                )
                value, turned = value.astype(BF16), turned.astype(BF16)
                backward[u, rows, 0:128] = value
                backward[u, low, 0:128] = turned
                if u > 0:
                    backward[u, rows, 128:256] = turned
                    backward[u, low, 128:256] = -value
        for m in range(4):
            rows = slice(128 * m, 128 * m + 128)
            left_side = fourier[rows, :]
            tw = twiddle[rows, :]
            terms = [dot(left_side, backward[0, :, 0:128])]
            for u in (1, 2, 3):
                both = dot(left_side, backward[u])
                cos, sin = tw[:, 2 * u - 2 : 2 * u - 1], tw[:, 2 * u - 1 : 2 * u]
                value, turned = both[:, 0:128], both[:, 128:256]
                terms.append(cos * value + sin * turned)
                if u == 1:
                    turned_odd = cos * turned - sin * value
                if u == 3:
                    turned_odd = turned_odd - (cos * turned - sin * value)
            plus, minus, odd = terms[0] + terms[2], terms[0] - terms[2], terms[1] + terms[3]
            for j, value in enumerate((plus + odd, minus + turned_odd, plus - odd, minus - turned_odd)):
                hsend[512 * j + 128 * m : 512 * j + 128 * m + 128, :] = value
        for k in range(15):
            h_copy(k).start()
        hrecv[me] = hsend[at(me, ROWS), :]

    for bank in range(BANKS):
        for copy in far_copies(bank):
            copy.wait_recv()
        low = pl.ds(pl.multiple_of(zp * QUARTER, QUARTER), 16)
        high = pl.ds(pl.multiple_of(zm * QUARTER + 16, 16), 16)
        squares[bank, low, :] = squares[bank, low, :] + far[bank, 0]
        squares[bank, high, :] = squares[bank, high, :] + far[bank, 1]
        for copy in near_copies(bank):
            copy.start()
    transform_columns()
    for bank in range(BANKS):
        for copy in near_copies(bank):
            copy.wait_recv()
        quarter_sum[bank] = squares[bank, at(z, QUARTER), :] + near[bank, 0] + near[bank, 1]
        x_copy(bank).start()
    swaps[5].start()

    bound = shrink_level * math.sqrt(8.0)
    for bank in range(BANKS):
        x_copy(bank).wait_recv()
        total = quarter_sum[bank] + other_sum[bank]
        factor[bank, at(z, QUARTER), :] = bound / jnp.maximum(jnp.sqrt(total), bound)
        for copy in gather_near(bank):
            copy.start()
    receive_swaps()
    transform_back()
    for bank in range(BANKS):
        for copy in gather_near(bank):
            copy.wait_recv()
        for copy in gather_far(bank):
            copy.start()

    dual_outs = []
    for bank in range(BANKS):
        for copy in gather_far(bank):
            copy.wait_recv()

        def shrink(i, bank=bank):
            rows = at(i, 16)
            fresh = (trial[bank, rows, :] * factor[bank, rows, :]).astype(BF16)
            dual_new[bank, rows, :] = fresh
            inner = pl.ds(pl.multiple_of(RIM + i * 16, 8), 16)
            combined[bank, inner, :] = 2.0 * fresh.astype(F32) - dual[bank, rows, :].astype(F32)

        loop(8, shrink)
        edge_send[bank, 0] = combined[bank, RIM : 2 * RIM]
        edge_send[bank, 1] = combined[bank, ROWS : RIM + ROWS]
        for copy in edge_copies(remote, bank, edge_send, edge_recv, edge_s, edge_r, before, after):
            copy.start()
    dual_copy = pltpu.make_async_copy(dual_new, dual_out, out_sem.at[0])
    dual_copy.start()

    for bank in range(BANKS):
        for copy in edge_copies(remote, bank, edge_send, edge_recv, edge_s, edge_r, before, after):
            copy.wait_recv()
        combined[bank, RIM + ROWS : PAD] = jnp.where(me == STRIPS - 1, 0.0, edge_recv[bank, 0])
        combined[bank, 0:RIM] = jnp.where(me == 0, 0.0, edge_recv[bank, 1])
    for i in (9, 10):
        loads[i].wait()
    for bank in range(BANKS):
        synth_wide[bank, :, 0:128] = jnp.zeros((ROWS, 128), BF16)
        synth_wide[bank, :, 128 + PIX : 256 + PIX] = jnp.zeros((ROWS, 128), BF16)

        def synthesise_rows(i, bank=bank):
            for t in range(4):
                start = i * 1024 + t * 256
                cols = pl.ds(pl.multiple_of(start, 256), 256)
                values = dot(syn_rows[bank], combined[bank, :, cols].astype(BF16))
                synth_wide[bank, :, pl.ds(pl.multiple_of(128 + start, 128), 256)] = values.astype(BF16)

        loop(2, synthesise_rows)

    def synthesise_columns(i):
        for t in range(4):
            start = pl.multiple_of(i * 512 + t * 128, 128)
            window = pl.ds(start, 384)
            adjoint[:, pl.ds(start, 128)] = dot(synth_wide[0, :, window], syn_cols[0:384]) + dot(
                synth_wide[1, :, window], syn_cols[384:768]
            )

    loop(4, synthesise_columns)

    for k in range(15):
        h_copy(k).wait_recv()
    for p in range(8):
        packed[0, :, 128 * p : 128 * p + 128] = hrecv[p].astype(BF16)
        packed[1, :, 128 * p : 128 * p + 128] = hrecv[15 - p].astype(BF16)

    def finish(i):
        cols = at(i, 256)
        even, odd = (
            lax.dot_general(packed[j], basis[j, cols, :], turn, preferred_element_type=F32)
            for j in range(2)
        )
        for gradient, where in (
            (even + odd, cols),
            (even - odd, pl.ds(pl.multiple_of(1024 + i * 256, 256), 256)),
        ):
            image_new[:, where] = xpad[RIM : RIM + ROWS, where] - tau_primal * (
                gradient + adjoint[:, where]
            )

    loop(4, finish)
    image_copy = pltpu.make_async_copy(image_new, image_out, out_sem.at[1])
    image_copy.start()

    for copy in halos:
        copy.wait_send()
    for k in range(15):
        y_copy(k).wait_send()
        h_copy(k).wait_send()
    for copy in swaps:
        copy.wait_send()
    for bank in range(BANKS):
        for copy in far_copies(bank) + near_copies(bank) + gather_near(bank) + gather_far(bank):
            copy.wait_send()
        x_copy(bank).wait_send()
        for copy in edge_copies(remote, bank, edge_send, edge_recv, edge_s, edge_r, before, after):
            copy.wait_send()
    dual_copy.wait()
    image_copy.wait()


def edge_copies(remote, bank, edge_send, edge_recv, edge_s, edge_r, before, after):
    return [
        remote(
            edge_send.at[bank, side], edge_recv.at[bank, side],
            edge_s.at[2 * bank + side], edge_r.at[2 * bank + side], (before, after)[side],
        )
        for side in range(2)
    ]


def clip_kernel(image_hbm, dual_hbm, image_out, dual_out, image, dual, in_sem, out_sem):
    parts = [
        (image_hbm.at[32 * i : 32 * i + 32], image.at[32 * i : 32 * i + 32], image_out.at[32 * i : 32 * i + 32])
        for i in range(4)
    ] + [
        (dual_hbm.at[b, 64 * i : 64 * i + 64], dual.at[b, 64 * i : 64 * i + 64], dual_out.at[b, 64 * i : 64 * i + 64])
        for b in range(2)
        for i in range(2)
    ]
    reads = [pltpu.make_async_copy(p[0], p[1], in_sem.at[i]) for i, p in enumerate(parts)]
    writes = [pltpu.make_async_copy(p[1], p[2], out_sem.at[i]) for i, p in enumerate(parts)]
    for read in reads:
        read.start()
    for i, (read, write) in enumerate(zip(reads, writes)):
        read.wait()
        if i < 4:
            image[32 * i : 32 * i + 32] = jnp.maximum(image[32 * i : 32 * i + 32], 0.0)
        write.start()
    for write in writes:
        write.wait()


def per_device(constants, image, dual_coeffs, block_ids, block_counts, block_weights, block_data):
    any_space = in_hbm = pl.BlockSpec(memory_space=pl.ANY)
    in_vmem = pl.BlockSpec(memory_space=pltpu.VMEM)
    dma = lambda *n: pltpu.SemaphoreType.DMA(n)
    vmem = pltpu.VMEM
    image_new, dual_new = pl.pallas_call(
        kernel,
        out_shape=(
            jax.ShapeDtypeStruct((ROWS, PIX), F32),
            jax.ShapeDtypeStruct((BANKS, ROWS, PIX), BF16),
        ),
        in_specs=[any_space, any_space, in_vmem, in_vmem] + [any_space] * 9,
        out_specs=(any_space, any_space),
        scratch_shapes=[
            vmem((PAD, PIX), F32),
            vmem((PAD, PIX + 256), BF16),
            vmem((BANKS, ROWS, PIX), BF16),
            vmem((32, 32, 128), BF16),
            vmem((2, 32, 32, 128), BF16),
            vmem((8, 32, 1024), F32),
            vmem((512, 1024), BF16),
            vmem((512, 128), F32),
            vmem((384, 256), BF16),
            vmem((BANKS, ROWS, PAD), BF16),
            vmem((BANKS, ROWS, PAD), BF16),
            vmem((768, 128), BF16),
            vmem((2, 1024, 1024), BF16),
            vmem((2, ROWS, 1024), BF16),
            vmem((STRIPS, ROWS, 128), F32),
            vmem((PIX, 128), F32),
            vmem((PIX, 128), F32),
            vmem((STRIPS, ROWS, 128), F32),
            vmem((BANKS, PAD, PIX), BF16),
            vmem((BANKS, ROWS, PIX), F32),
            vmem((BANKS, ROWS, PIX), F32),
            vmem((BANKS, 2, QUARTER, PIX), F32),
            vmem((BANKS, 2, 16, PIX), F32),
            vmem((BANKS, QUARTER, PIX), F32),
            vmem((BANKS, QUARTER, PIX), F32),
            vmem((BANKS, ROWS, PIX), F32),
            vmem((BANKS, PAD, PIX), F32),
            vmem((BANKS, 2, RIM, PIX), F32),
            vmem((BANKS, 2, RIM, PIX), F32),
            vmem((BANKS, ROWS, PIX + 256), BF16),
            vmem((ROWS, PIX), F32),
            vmem((2, 1024, 128), F32),
            vmem((1024, 128), F32),
            vmem((2, 1024, 128), F32),
            vmem((512, 128), F32),
            vmem((512, 128), F32),
            vmem((1024, 128), F32),
            vmem((1024, 128), F32),
            vmem((8, 256), F32),
            vmem((2, 8, 256), F32),
            vmem((8, 1024), F32),
            vmem((8, 1024), F32),
            vmem((2, 2, 4, 512, 128), BF16),
            vmem((4, 1024, 256), BF16),
            vmem((2, 4, 512, 128), F32),
            vmem((4, 1024, 256), BF16),
            vmem((2, ROWS, 1024), BF16),
            vmem((ROWS, PIX), F32),
            vmem((BANKS, ROWS, PIX), BF16),
            dma(11), dma(15), dma(15), dma(15), dma(15), dma(2), dma(2), dma(4), dma(4),
            dma(4), dma(4), dma(4), dma(4), dma(2), dma(2), dma(4), dma(4), dma(4), dma(4), dma(6), dma(6), dma(2),
        ],
        compiler_params=pltpu.CompilerParams(
            collective_id=0, has_side_effects=True, vmem_limit_bytes=60 * 1024 * 1024
        ),
    )(
        image[0],
        dual_coeffs[:, 0],
        block_ids,
        block_counts,
        block_weights[0],
        block_data[0],
        *constants,
    )
    image_new, dual_new = pl.pallas_call(
        clip_kernel,
        out_shape=(
            jax.ShapeDtypeStruct((ROWS, PIX), F32),
            jax.ShapeDtypeStruct((BANKS, ROWS, PIX), BF16),
        ),
        in_specs=[in_hbm, in_hbm],
        out_specs=(in_hbm, in_hbm),
        scratch_shapes=[vmem((ROWS, PIX), F32), vmem((BANKS, ROWS, PIX), BF16), dma(8), dma(8)],
        compiler_params=pltpu.CompilerParams(vmem_limit_bytes=60 * 1024 * 1024),
    )(image_new, dual_new)
    return image_new[None], dual_new[:, None]


def solution(mesh):
    constants = tuple(jnp.asarray(c) for c in make_constants())

    def body(*args):
        return per_device(constants, *args)

    return jax.shard_map(
        body,
        mesh=mesh,
        in_specs=(
            P("chan", "strip", None),
            P(None, "chan", "strip", None),
            P("chan", "strip"),
            P("chan", "strip"),
            P("chan", "strip", None, None),
            P("chan", None, "strip", None, None),
        ),
        out_specs=(P("chan", "strip", None), P(None, "chan", "strip", None)),
        check_vma=False,
    )
```

```python
import math

import jax
import jax.numpy as jnp
import numpy as np
from jax import lax
from jax.experimental import pallas as pl
from jax.experimental.pallas import tpu as pltpu
from jax.sharding import PartitionSpec as P

MESH = pl.DeviceIdType.MESH
F32, BF16 = jnp.float32, jnp.bfloat16

PIX = 2048
ROWS = 128
STRIPS = 16
RIM = 8
PAD = ROWS + 2 * RIM
BANKS = 2
QUARTER = ROWS // 4
CHUNKS = 4
FAR_FIRST = [
    (dx, dy, core)
    for dx, dy in ((1, 2), (0, 2), (1, 1), (1, 3), (0, 1), (0, 3), (1, 0))
    for core in (0, 1)
] + [(0, 0, 1)]

root_three = math.sqrt(3.0)
sqrt_two = math.sqrt(2.0)
daub_two = [
    (1.0 + root_three) / (4.0 * sqrt_two),
    (3.0 + root_three) / (4.0 * sqrt_two),
    (3.0 - root_three) / (4.0 * sqrt_two),
    (1.0 - root_three) / (4.0 * sqrt_two),
]
daub_four = [
    0.2303778133088964,
    0.7148465705529155,
    0.6308807679298587,
    -0.0279837694168599,
    -0.1870348117190931,
    0.0308413818355607,
    0.0328830116668852,
    -0.010597401785069,
]
bank_filters = [daub_two, daub_four]
sigma_dual = 0.5
tau_primal = 0.3
shrink_level = 0.5


def bank_matrix(taps, out_at, out_count, in_at, in_count):
    count = len(taps)
    high = [(-1) ** k * taps[count - 1 - k] for k in range(count)]
    offset = count // 2 - 1
    matrix = np.zeros((out_count, in_count), np.float64)
    for i in range(out_count):
        m = out_at + i
        even = m - m % 2
        for k in range(count):
            n = even + k - offset - in_at
            if 0 <= n < in_count:
                matrix[i, n] = (taps if m % 2 == 0 else high)[k]
    return matrix


def make_constants():
    two_pi = 2.0 * math.pi
    tables = []
    for parity in range(2):
        tile, part, k = np.meshgrid(np.arange(8), np.arange(2), np.arange(64), indexing="ij")
        freq = 128 * tile + 2 * k + parity
        phase = part * (math.pi / 2)
        if parity == 0:
            freq[0, 1, 0] = PIX // 2
            phase = phase.copy()
            phase[0, 1, 0] = 0.0
        freq, phase = freq.reshape(-1), phase.reshape(-1)
        coarse = two_pi * (32 * np.arange(32)[:, None] * freq[None, :] % PIX) / PIX
        fine = two_pi * (np.arange(32)[:, None] * freq[None, :] % PIX) / PIX + phase[None, :]
        tables += [np.cos(coarse), np.sin(coarse), np.cos(fine) / 32.0, np.sin(fine) / 32.0]
    tables = np.stack(tables).astype(np.float32)
    grid = two_pi * (np.arange(512)[:, None] * np.arange(512)[None, :] % 512) / 512
    fourier = np.concatenate([np.cos(grid), np.sin(grid)], axis=1) / 64.0
    twiddle = np.zeros((512, 128), np.float32)
    for u in (1, 2, 3):
        angle = two_pi * (np.arange(512) * u) / PIX
        twiddle[:, 2 * u - 2] = np.cos(angle)
        twiddle[:, 2 * u - 1] = np.sin(angle)
    ana_cols = np.concatenate(
        [bank_matrix(t, 128, 128, 0, 384).T for t in bank_filters], axis=1
    )
    ana_rows = np.stack([sigma_dual * bank_matrix(t, RIM, ROWS, 0, PAD) for t in bank_filters])
    syn_all = np.stack([bank_matrix(t, 0, PAD, RIM, ROWS).T for t in bank_filters])
    syn_rows = syn_all[:, :, RIM : RIM + ROWS]
    rims = np.concatenate([syn_all[:, :, 0:RIM], syn_all[:, :, RIM + ROWS :]], axis=2)
    syn_rims = np.concatenate([rims[:, 0:16], rims[:, ROWS - 16 :]], axis=1)
    syn_cols = np.concatenate([bank_matrix(t, 0, 384, 128, 128) for t in bank_filters], axis=0)
    as_bf16 = lambda a: np.asarray(a, np.float32).astype(BF16)
    return (
        tables,
        as_bf16(fourier),
        twiddle,
        as_bf16(ana_cols),
        as_bf16(ana_rows),
        as_bf16(syn_rows),
        as_bf16(syn_rims),
        as_bf16(syn_cols),
    )


def dot(a, b):
    return jnp.dot(a, b, preferred_element_type=F32)


def lanes(shape):
    return lax.broadcasted_iota(jnp.int32, shape, len(shape) - 1)


def loop(count, body):
    def step(i, carry):
        body(i)
        return carry

    lax.fori_loop(0, count, step, 0)


def peer_at(me, k):
    dx, dy, core = FAR_FIRST[k]
    return ((me // 8 + dx) % 2) * 8 + (((me // 2) % 4 + dy) % 4) * 2 + (me + core) % 2


def at(i, width):
    return pl.ds(pl.multiple_of(i * width, width), width)


def kernel(
    image_hbm, dual_hbm, ids_ref, counts_ref, weights_hbm, data_hbm,
    tables_hbm, fourier_hbm, twiddle_hbm, ana_cols_hbm, ana_rows_hbm, syn_rows_hbm, syn_rims_hbm, syn_cols_hbm,
    image_out, dual_out,
    xpad, xwide, dual, weights, data, tables, fourier, twiddle, ana_cols, ana_rows, syn_rows, syn_rims, syn_cols,
    basis, folded, ysend, yrecv, hsend, hrecv, coeffs, trial, squares, near, far, quarter_sum, other_sum,
    factor, combined, edge_send, edge_recv, synth_wide, adjoint, own_flat, other_flat, rim_flat,
    w_send, w_recv, d_send, d_recv, ids_send, ids_recv, rim_send, rim_recv, wd_dense,
    forward, kept, backward, packed, image_new, dual_new,
    local_sem, y_s, y_r, h_s, h_r, halo_s, halo_r, edge_s, edge_r, far_s, far_r, near_s, near_r,
    x_s, x_r, ga_s, ga_r, gb_s, gb_r, swap_s, swap_r, out_sem,
):
    me = lax.axis_index("strip")
    chan = lax.axis_index("chan")
    z = chan % 4
    x_hi = chan // 4
    zp, zm, zf = (z + 1) % 4, (z + 3) % 4, (z + 2) % 4
    up = {"chan": x_hi * 4 + zp}
    down = {"chan": x_hi * 4 + zm}
    across = {"chan": (1 - x_hi) * 4 + z}
    before, after = {"strip": (me + 15) % STRIPS}, {"strip": (me + 1) % STRIPS}
    sign = jnp.where(me < 8, 1, -1)

    sources = {
        "weights": (weights_hbm, weights),
        "data": (data_hbm, data),
        "image": (image_hbm, xpad.at[RIM : RIM + ROWS]),
        "tables": (tables_hbm, tables),
        "ana_cols": (ana_cols_hbm, ana_cols),
        "ana_rows": (ana_rows_hbm, ana_rows),
        "dual": (dual_hbm, dual),
        "fourier": (fourier_hbm, fourier),
        "twiddle": (twiddle_hbm, twiddle),
        "syn_rows": (syn_rows_hbm, syn_rows),
        "syn_rims": (syn_rims_hbm, syn_rims),
        "syn_cols": (syn_cols_hbm, syn_cols),
    }
    loads = {
        name: pltpu.make_async_copy(src, dst, local_sem.at[i])
        for i, (name, (src, dst)) in enumerate(sources.items())
    }
    for load in loads.values():
        load.start()

    barrier = pltpu.get_barrier_semaphore()
    for k in range(1, STRIPS):
        pl.semaphore_signal(
            barrier, inc=1, device_id={"strip": (me + k) % STRIPS}, device_id_type=MESH
        )
    for peer in (up, down, across):
        pl.semaphore_signal(barrier, inc=1, device_id=peer, device_id_type=MESH)
    def remote(src, dst, send, recv, peer):
        return pltpu.make_async_remote_copy(
            src_ref=src, dst_ref=dst, send_sem=send, recv_sem=recv, device_id=peer, device_id_type=MESH
        )

    loads["weights"].wait()
    loads["data"].wait()
    lane_of = lanes((128, 128))
    half_lane = lane_of % 64
    imag_lane = lane_of >= 64
    column_row = lax.broadcasted_iota(jnp.int32, (128, 128), 0)
    own_hit = column_row == jnp.where(me < 8, 2 * half_lane, 127 - 2 * half_lane)
    other_hit = column_row == jnp.where(me < 8, 2 * half_lane + 1, 128 - 2 * half_lane)
    one_hot = lambda mask: jnp.where(mask, 1.0, 0.0).astype(BF16)
    signed = lambda mask: jnp.where(mask, sign.astype(F32), 0.0).astype(BF16)
    own_real, own_imag = one_hot(own_hit & ~imag_lane), signed(own_hit & imag_lane)
    other_real, other_imag = one_hot(other_hit & ~imag_lane), signed(other_hit & imag_lane)
    other_low, other_high = one_hot(other_hit & ~imag_lane), one_hot(other_hit & imag_lane)
    mirror = {"strip": 15 - me}
    rim_peer = {"strip": jnp.where(me < 8, 8 + (8 - me) % 8, (16 - me) % 8)}

    def picked_rows(ref, i):
        return ref[8 * i : 8 * i + 8].reshape(256, 128)

    for i in range(4):
        rows = slice(256 * i, 256 * i + 256)
        d_send[rows, :] = dot(picked_rows(data.at[0], i), other_real) + dot(
            picked_rows(data.at[1], i), other_imag
        )
        if i < 2:
            w_send[rows, :] = dot(picked_rows(weights, i), other_low) + dot(
                picked_rows(weights, i + 2), other_high
            )
    slot = lanes((8, 32))
    ids = jnp.broadcast_to(ids_ref[...], (8, 32))
    live_ids = jnp.where(slot < counts_ref[...], ids, -1).astype(F32).astype(BF16)
    spread = jnp.where(
        lanes((32, 256)) // 8 == lax.broadcasted_iota(jnp.int32, (32, 256), 0), 1.0, 0.0
    ).astype(BF16)
    ids_send[...] = dot(live_ids, spread)
    sel_row, sel_lane = lax.broadcasted_iota(jnp.int32, (8, 128), 0), lanes((8, 128))
    turn = (((1,), (1,)), ((), ()))
    rim = 0.0
    for i, values in enumerate((weights[...], data[0], data[1])):
        select = one_hot((sel_row == i) & (sel_lane == 0))
        rim = rim + lax.dot_general(select, values.reshape(1024, 128), turn, preferred_element_type=F32)
    rim_send[...] = rim
    pl.semaphore_wait(barrier, STRIPS + 2)

    halos = [
        remote(xpad.at[RIM : 2 * RIM], xpad.at[RIM + ROWS : PAD], halo_s.at[0], halo_r.at[0], before),
        remote(xpad.at[ROWS : RIM + ROWS], xpad.at[0:RIM], halo_s.at[1], halo_r.at[1], after),
    ]
    loads["image"].wait()
    for copy in halos:
        copy.start()
    swaps = [
        remote(w_send, w_recv, swap_s.at[0], swap_r.at[0], mirror),
        remote(ids_send, ids_recv.at[0], swap_s.at[1], swap_r.at[1], mirror),
        remote(ids_send, ids_recv.at[1], swap_s.at[2], swap_r.at[2], rim_peer),
        remote(rim_send, rim_recv, swap_s.at[3], swap_r.at[3], rim_peer),
        remote(d_send, d_recv, swap_s.at[4], swap_r.at[4], mirror),
    ]
    for copy in swaps:
        copy.start()

    loads["tables"].wait()
    for parity in range(2):
        def make_basis(i, parity=parity):
            coarse_cos = tables[4 * parity, pl.ds(i, 1), :]
            coarse_sin = tables[4 * parity + 1, pl.ds(i, 1), :]
            block = coarse_cos * tables[4 * parity + 2] - coarse_sin * tables[4 * parity + 3]
            basis[parity, at(i, 32), :] = block.astype(BF16)

        loop(32, make_basis)
    left, right = xpad[RIM : RIM + ROWS, 0:1024], xpad[RIM : RIM + ROWS, 1024:2048]
    folded[0] = (left + right).astype(BF16)
    folded[1] = (left - right).astype(BF16)
    def y_copy(k):
        q = peer_at(me, k)
        return remote(ysend.at[q], yrecv.at[at(me, ROWS)], y_s.at[k], y_r.at[k], {"strip": q})

    for e in range(2):
        for pair in range(4):
            tiles = dot(folded[e], basis[e, :, 256 * pair : 256 * pair + 256])
            for half in range(2):
                p = 2 * pair + half
                ysend[15 - p if e else p] = tiles[:, 128 * half : 128 * half + 128]
    for k in range(15):
        y_copy(k).start()
    yrecv[at(me, ROWS), :] = ysend[me]

    for copy in halos:
        copy.wait_recv()
    for name in ("ana_cols", "ana_rows", "dual"):
        loads[name].wait()
    xwide[:, 0:128] = jnp.zeros((PAD, 128), BF16)
    xwide[:, 128 + PIX : 256 + PIX] = jnp.zeros((PAD, 128), BF16)
    row = lax.broadcasted_iota(jnp.int32, (PAD, PIX), 0)
    outside = ((row < RIM) & (me == 0)) | ((row >= RIM + ROWS) & (me == STRIPS - 1))
    xwide[:, 128 : 128 + PIX] = jnp.where(outside, 0.0, xpad[...]).astype(BF16)

    def analyse_columns(i):
        for t in range(4):
            start = pl.multiple_of(i * 512 + t * 128, 128)
            both = dot(xwide[:, pl.ds(start, 384)], ana_cols[...]).astype(BF16)
            coeffs[0, :, pl.ds(start, 128)] = both[:, 0:128]
            coeffs[1, :, pl.ds(start, 128)] = both[:, 128:256]

    loop(4, analyse_columns)

    def cols_of(c):
        return slice(1024 * (c % 2), 1024 * (c % 2) + 1024)

    def far_copies(c):
        bank, cols = c // 2, cols_of(c)
        low = pl.ds(pl.multiple_of(zf * QUARTER, QUARTER), 16)
        high = pl.ds(pl.multiple_of(zf * QUARTER + 16, 16), 16)
        return [
            remote(squares.at[bank, low, cols], far.at[bank, 0, :, cols], far_s.at[c, 0], far_r.at[c, 0], up),
            remote(squares.at[bank, high, cols], far.at[bank, 1, :, cols], far_s.at[c, 1], far_r.at[c, 1], down),
        ]

    def near_copies(c):
        bank, cols = c // 2, cols_of(c)
        return [
            remote(
                squares.at[bank, at(where, QUARTER), cols], near.at[bank, side, :, cols],
                near_s.at[c, side], near_r.at[c, side], peer,
            )
            for side, (where, peer) in enumerate(((zp, up), (zm, down)))
        ]

    def x_copy(c):
        bank, cols = c // 2, cols_of(c)
        return remote(
            quarter_sum.at[bank, :, cols], other_sum.at[bank, :, cols], x_s.at[c], x_r.at[c], across
        )

    def gather_near(c):
        mine = factor.at[c // 2, at(z, QUARTER), cols_of(c)]
        return [
            remote(mine, mine, ga_s.at[c, side], ga_r.at[c, side], peer)
            for side, peer in enumerate((up, down))
        ]

    def gather_far(c):
        low = factor.at[c // 2, pl.ds(pl.multiple_of(zm * QUARTER, QUARTER), 16), cols_of(c)]
        high = factor.at[c // 2, pl.ds(pl.multiple_of(zp * QUARTER + 16, 16), 16), cols_of(c)]
        return [
            remote(low, low, gb_s.at[c, 0], gb_r.at[c, 0], up),
            remote(high, high, gb_s.at[c, 1], gb_r.at[c, 1], down),
        ]

    def edge_copies(c):
        cols = cols_of(c)
        return [
            remote(
                edge_send.at[c // 2, side, :, cols], edge_recv.at[c // 2, side, :, cols],
                edge_s.at[c, side], edge_r.at[c, side], peer,
            )
            for side, peer in enumerate((before, after))
        ]

    for c in range(CHUNKS):
        bank = c // 2
        for t in range(4):
            cols = slice(1024 * (c % 2) + 256 * t, 1024 * (c % 2) + 256 * t + 256)
            values = dual[bank, :, cols].astype(F32) + dot(ana_rows[bank], coeffs[bank, :, cols])
            trial[bank, :, cols] = values
            squares[bank, :, cols] = values * values
        for copy in far_copies(c):
            copy.start()

    for i in range(4):
        rows = slice(256 * i, 256 * i + 256)
        own_flat[0, rows, :] = dot(picked_rows(weights, i), one_hot(own_hit))
        own_flat[1, rows, :] = dot(picked_rows(data.at[0], i), own_real) + dot(
            picked_rows(data.at[1], i), own_imag
        )
    place_row = lax.broadcasted_iota(jnp.int32, (512, 256), 0)
    same_row = place_row % 8 == lanes((512, 256)) % 8

    def place_of(slot_ids):
        return one_hot((slot_ids[0:1, :].astype(jnp.int32) == place_row // 8) & same_row)

    def by_row(flat_w, flat_d, u):
        rows = pl.ds(u, 256, stride=4)
        return jnp.concatenate([flat_w[rows, :], flat_d[rows, :]], axis=1).astype(BF16)

    def put_dense(role, u, values):
        values = values.astype(BF16)
        wd_dense[role, 0, u] = values[:, 0:128]
        wd_dense[role, 1, u] = values[:, 128:256]

    own_place = place_of(ids_send[...])
    for u in range(4):
        put_dense(0, u, dot(own_place, by_row(own_flat.at[0], own_flat.at[1], u)))

    lane_sign = jnp.where(lanes((1, 128)) < 64, -sign, sign).astype(F32)
    swap_halves = lambda values: pltpu.roll(values, 64, 1)
    first_lane = (lanes((1, 128)) == 0) & (me == 0)
    middle_lane = (lanes((1, 128)) == 64) & (me == 0)

    def times_i(values):
        return lane_sign * swap_halves(values)

    def h_copy(k):
        q = peer_at(me, k)
        return remote(hsend.at[at(q, ROWS)], hrecv.at[me], h_s.at[k], h_r.at[k], {"strip": q})

    def fold_rows(i):
        for part in range(2):
            start = i * 128 + part * 64
            rows = pl.ds(pl.multiple_of(start, 64), 64)
            low = pl.ds(pl.multiple_of(512 + start, 64), 64)
            loaded = [yrecv[pl.ds(pl.multiple_of(512 * j + start, 64), 64), :] for j in range(4)]
            tw = twiddle[rows, :]
            for role in range(2):
                if role == 0:
                    parts = [jnp.where(middle_lane, 0.0, y) for y in loaded]
                else:
                    parts = [
                        jnp.where(first_lane, swap_halves(y), jnp.where(middle_lane, 0.0, y)) for y in loaded
                    ]
                unit = times_i if role == 0 else (lambda values: -times_i(values))
                y0, y1, y2, y3 = parts
                sum_a, sum_b, dif_a, dif_b = y0 + y2, y1 + y3, y0 - y2, y1 - y3
                total, alt = sum_a + sum_b, sum_a - sum_b
                turned_a, turned_b = unit(dif_a), unit(dif_b)
                folds = (
                    (total, unit(total)),
                    (dif_a - turned_b, turned_a + dif_b),
                    (alt, unit(alt)),
                    (dif_a + turned_b, turned_a - dif_b),
                )
                lanes_of = slice(128 * role, 128 * role + 128)
                for u, (value, turned) in enumerate(folds):
                    if u > 0:
                        cos, sin = tw[:, 2 * u - 2 : 2 * u - 1], tw[:, 2 * u - 1 : 2 * u]
                        value, turned = cos * value - sin * turned, cos * turned + sin * value
                    forward[u, rows, lanes_of] = value.astype(BF16)
                    forward[u, low, lanes_of] = (-turned).astype(BF16)

    def weigh(role, u, rows, spectrum):
        weight = wd_dense[role, 0, u, rows, :].astype(F32)
        return weight * (weight * spectrum - wd_dense[role, 1, u, rows, :].astype(F32))

    def transform_columns():
        for k in range(15):
            y_copy(k).wait_recv()
        loop(4, fold_rows)
        for u in range(4):
            for m in range(2):
                rows = slice(256 * m, 256 * m + 256)
                both = dot(fourier[rows, :], forward[u])
                kept[0, u, rows, :] = weigh(0, u, rows, both[:, 0:128])
                kept[1, u, rows, :] = both[:, 128:256]

    def receive_swaps():
        for copy in swaps:
            copy.wait_recv()
        for m in range(2):
            rows = slice(256 * m, 256 * m + 256)
            values = w_recv[rows, :]
            turned = swap_halves(values)
            left_lane = lanes((256, 128)) < 64
            other_flat[256 * m : 256 * m + 256, :] = jnp.where(left_lane, values, turned)
            other_flat[512 + 256 * m : 768 + 256 * m, :] = jnp.where(left_lane, turned, values)
        rims = jnp.concatenate([rim_recv[...], jnp.zeros((120, 1024), F32)], axis=0).T.astype(BF16)
        has_rim = me < 8
        rim_w = one_hot((column_row == 0) & (half_lane == 0) & has_rim)
        rim_d = one_hot((column_row == 1) & (lane_of == 0) & has_rim) - one_hot(
            (column_row == 2) & (lane_of == 64) & has_rim
        )
        rim_flat[0] = dot(rims, rim_w)
        rim_flat[1] = dot(rims, rim_d)
        other_place, rim_place = place_of(ids_recv[0]), place_of(ids_recv[1])
        for u in range(4):
            put_dense(
                1, u,
                dot(other_place, by_row(other_flat, d_recv, u))
                + dot(rim_place, by_row(rim_flat.at[0], rim_flat.at[1], u)),
            )

    def transform_back():
        for u in range(4):
            for m in range(2):
                rows, low = slice(256 * m, 256 * m + 256), slice(512 + 256 * m, 768 + 256 * m)
                own, other = kept[0, u, rows, :], weigh(1, u, rows, kept[1, u, rows, :])
                own_turned, other_swapped = times_i(own), swap_halves(other)
                value = jnp.where(first_lane, own, jnp.where(middle_lane, other_swapped, own + other))
                turned = jnp.where(
                    first_lane, own_turned,
                    jnp.where(middle_lane, other, own_turned - lane_sign * other_swapped),
                )
                value, turned = value.astype(BF16), turned.astype(BF16)
                backward[u, rows, 0:128] = value
                backward[u, low, 0:128] = turned
                if u > 0:
                    backward[u, rows, 128:256] = turned
                    backward[u, low, 128:256] = -value
        for m in range(4):
            rows = slice(128 * m, 128 * m + 128)
            left_side = fourier[rows, :]
            tw = twiddle[rows, :]
            terms = [dot(left_side, backward[0, :, 0:128])]
            for u in (1, 2, 3):
                both = dot(left_side, backward[u])
                cos, sin = tw[:, 2 * u - 2 : 2 * u - 1], tw[:, 2 * u - 1 : 2 * u]
                value, turned = both[:, 0:128], both[:, 128:256]
                terms.append(cos * value + sin * turned)
                if u == 1:
                    turned_odd = cos * turned - sin * value
                if u == 3:
                    turned_odd = turned_odd - (cos * turned - sin * value)
            plus, minus, odd = terms[0] + terms[2], terms[0] - terms[2], terms[1] + terms[3]
            for j, value in enumerate((plus + odd, minus + turned_odd, plus - odd, minus - turned_odd)):
                hsend[512 * j + 128 * m : 512 * j + 128 * m + 128, :] = value
        for k in range(15):
            h_copy(k).start()
        hrecv[me] = hsend[at(me, ROWS), :]

    def send_near(c):
        bank, cols = c // 2, cols_of(c)
        for copy in far_copies(c):
            copy.wait_recv()
        low = pl.ds(pl.multiple_of(zp * QUARTER, QUARTER), 16)
        high = pl.ds(pl.multiple_of(zm * QUARTER + 16, 16), 16)
        squares[bank, low, cols] = squares[bank, low, cols] + far[bank, 0, :, cols]
        squares[bank, high, cols] = squares[bank, high, cols] + far[bank, 1, :, cols]
        for copy in near_copies(c):
            copy.start()

    def send_across(c):
        bank, cols = c // 2, cols_of(c)
        for copy in near_copies(c):
            copy.wait_recv()
        quarter_sum[bank, :, cols] = (
            squares[bank, at(z, QUARTER), cols] + near[bank, 0, :, cols] + near[bank, 1, :, cols]
        )
        x_copy(c).start()

    bound = shrink_level * math.sqrt(8.0)

    def send_factor(c):
        bank, cols = c // 2, cols_of(c)
        x_copy(c).wait_recv()
        total = quarter_sum[bank, :, cols] + other_sum[bank, :, cols]
        factor[bank, at(z, QUARTER), cols] = bound / jnp.maximum(jnp.sqrt(total), bound)
        for copy in gather_near(c):
            copy.start()

    def pass_factor(c):
        for copy in gather_near(c):
            copy.wait_recv()
        for copy in gather_far(c):
            copy.start()

    def shrink(c):
        bank, cols = c // 2, cols_of(c)
        for copy in gather_far(c):
            copy.wait_recv()
        for i in range(8):
            rows = slice(16 * i, 16 * i + 16)
            fresh = (trial[bank, rows, cols] * factor[bank, rows, cols]).astype(BF16)
            dual_new[bank, rows, cols] = fresh
            values = 2.0 * fresh.astype(F32) - dual[bank, rows, cols].astype(F32)
            combined[bank, rows, cols] = values.astype(BF16)
            if i == 0:
                edge_send[bank, 0, :, cols] = values[0:RIM]
            if i == 7:
                edge_send[bank, 1, :, cols] = values[16 - RIM : 16]
        for copy in edge_copies(c):
            copy.start()

    def synthesise_rows(c):
        bank = c // 2
        for t in range(4):
            start = 1024 * (c % 2) + 256 * t
            values = dot(syn_rows[bank], combined[bank, :, start : start + 256])
            synth_wide[bank, :, 128 + start : 384 + start] = values.astype(BF16)

    def add_edges(c):
        bank, cols = c // 2, cols_of(c)
        wide = slice(128 + 1024 * (c % 2), 1152 + 1024 * (c % 2))
        for copy in edge_copies(c):
            copy.wait_recv()
        below = jnp.where(me == STRIPS - 1, 0.0, edge_recv[bank, 0, :, cols])
        above = jnp.where(me == 0, 0.0, edge_recv[bank, 1, :, cols])
        extra = dot(syn_rims[bank], jnp.concatenate([above, below], axis=0).astype(BF16))
        for rows, part in ((slice(0, 16), extra[0:16]), (slice(ROWS - 16, ROWS), extra[16:32])):
            synth_wide[bank, rows, wide] = (synth_wide[bank, rows, wide].astype(F32) + part).astype(BF16)

    def synthesise_columns(i, rows):
        for t in range(4):
            start = pl.multiple_of(i * 512 + t * 128, 128)
            window = pl.ds(start, 384)
            adjoint[rows, pl.ds(start, 128)] = dot(synth_wide[0, rows, window], syn_cols[0:384]) + dot(
                synth_wide[1, rows, window], syn_cols[384:768]
            )

    inner, outer = slice(16, ROWS - 16), (slice(0, 16), slice(ROWS - 16, ROWS))

    for c in range(CHUNKS):
        send_near(c)
    for name in ("fourier", "twiddle", "syn_rows", "syn_rims", "syn_cols"):
        loads[name].wait()
    for bank in range(BANKS):
        synth_wide[bank, :, 0:128] = jnp.zeros((ROWS, 128), BF16)
        synth_wide[bank, :, 128 + PIX : 256 + PIX] = jnp.zeros((ROWS, 128), BF16)
    send_across(0)
    send_across(1)
    send_across(2)
    send_across(3)
    transform_columns()
    send_factor(0)
    send_factor(1)
    send_factor(2)
    receive_swaps()
    transform_back()
    send_factor(3)
    pass_factor(0)
    pass_factor(1)
    pass_factor(2)
    pass_factor(3)
    shrink(0)
    synthesise_rows(0)
    shrink(1)
    synthesise_rows(1)
    shrink(2)
    synthesise_rows(2)
    shrink(3)
    synthesise_rows(3)
    dual_copy = pltpu.make_async_copy(dual_new, dual_out, out_sem.at[0])
    dual_copy.start()
    loop(4, lambda i: synthesise_columns(i, inner))
    for c in range(CHUNKS):
        add_edges(c)
    loop(4, lambda i: [synthesise_columns(i, rows) for rows in outer])

    for k in range(15):
        h_copy(k).wait_recv()
    for p in range(8):
        packed[0, :, 128 * p : 128 * p + 128] = hrecv[p].astype(BF16)
        packed[1, :, 128 * p : 128 * p + 128] = hrecv[15 - p].astype(BF16)

    def finish(i):
        cols = at(i, 256)
        even, odd = (
            lax.dot_general(packed[j], basis[j, cols, :], turn, preferred_element_type=F32)
            for j in range(2)
        )
        for gradient, where in (
            (even + odd, cols),
            (even - odd, pl.ds(pl.multiple_of(1024 + i * 256, 256), 256)),
        ):
            image_new[:, where] = xpad[RIM : RIM + ROWS, where] - tau_primal * (
                gradient + adjoint[:, where]
            )

    def image_copies(i):
        return [
            pltpu.make_async_copy(image_new.at[:, cols], image_out.at[:, cols], out_sem.at[1 + 2 * i + side])
            for side, cols in enumerate(
                (at(i, 256), pl.ds(pl.multiple_of(1024 + i * 256, 256), 256))
            )
        ]

    def finish_and_send(i):
        finish(i)
        for copy in image_copies(i):
            copy.start()

    loop(4, finish_and_send)

    for copy in halos:
        copy.wait_send()
    for k in range(15):
        y_copy(k).wait_send()
        h_copy(k).wait_send()
    for copy in swaps:
        copy.wait_send()
    for c in range(CHUNKS):
        for copy in far_copies(c) + near_copies(c) + gather_near(c) + gather_far(c) + edge_copies(c):
            copy.wait_send()
        x_copy(c).wait_send()
    dual_copy.wait()
    for i in range(4):
        for copy in image_copies(i):
            copy.wait()


def clip_kernel(image_hbm, dual_hbm, image_out, dual_out, image, dual, in_sem, out_sem):
    parts = [
        (image_hbm.at[32 * i : 32 * i + 32], image.at[32 * i : 32 * i + 32], image_out.at[32 * i : 32 * i + 32])
        for i in range(4)
    ] + [
        (dual_hbm.at[b, 64 * i : 64 * i + 64], dual.at[b, 64 * i : 64 * i + 64], dual_out.at[b, 64 * i : 64 * i + 64])
        for b in range(2)
        for i in range(2)
    ]
    reads = [pltpu.make_async_copy(p[0], p[1], in_sem.at[i]) for i, p in enumerate(parts)]
    writes = [pltpu.make_async_copy(p[1], p[2], out_sem.at[i]) for i, p in enumerate(parts)]
    for read in reads:
        read.start()
    for i, (read, write) in enumerate(zip(reads, writes)):
        read.wait()
        if i < 4:
            image[32 * i : 32 * i + 32] = jnp.maximum(image[32 * i : 32 * i + 32], 0.0)
        write.start()
    for write in writes:
        write.wait()


def per_device(constants, image, dual_coeffs, block_ids, block_counts, block_weights, block_data):
    any_space = in_hbm = pl.BlockSpec(memory_space=pl.ANY)
    in_vmem = pl.BlockSpec(memory_space=pltpu.VMEM)
    dma = lambda *n: pltpu.SemaphoreType.DMA(n)
    vmem = pltpu.VMEM
    image_new, dual_new = pl.pallas_call(
        kernel,
        out_shape=(
            jax.ShapeDtypeStruct((ROWS, PIX), F32),
            jax.ShapeDtypeStruct((BANKS, ROWS, PIX), BF16),
        ),
        in_specs=[any_space, any_space, in_vmem, in_vmem] + [any_space] * 10,
        out_specs=(any_space, any_space),
        scratch_shapes=[
            vmem((PAD, PIX), F32),
            vmem((PAD, PIX + 256), BF16),
            vmem((BANKS, ROWS, PIX), BF16),
            vmem((32, 32, 128), BF16),
            vmem((2, 32, 32, 128), BF16),
            vmem((8, 32, 1024), F32),
            vmem((512, 1024), BF16),
            vmem((512, 128), F32),
            vmem((384, 256), BF16),
            vmem((BANKS, ROWS, PAD), BF16),
            vmem((BANKS, ROWS, ROWS), BF16),
            vmem((BANKS, 32, 2 * RIM), BF16),
            vmem((768, 128), BF16),
            vmem((2, 1024, 1024), BF16),
            vmem((2, ROWS, 1024), BF16),
            vmem((STRIPS, ROWS, 128), F32),
            vmem((PIX, 128), F32),
            vmem((PIX, 128), F32),
            vmem((STRIPS, ROWS, 128), F32),
            vmem((BANKS, PAD, PIX), BF16),
            vmem((BANKS, ROWS, PIX), F32),
            vmem((BANKS, ROWS, PIX), F32),
            vmem((BANKS, 2, QUARTER, PIX), F32),
            vmem((BANKS, 2, 16, PIX), F32),
            vmem((BANKS, QUARTER, PIX), F32),
            vmem((BANKS, QUARTER, PIX), F32),
            vmem((BANKS, ROWS, PIX), F32),
            vmem((BANKS, ROWS, PIX), BF16),
            vmem((BANKS, 2, RIM, PIX), F32),
            vmem((BANKS, 2, RIM, PIX), F32),
            vmem((BANKS, ROWS, PIX + 256), BF16),
            vmem((ROWS, PIX), F32),
            vmem((2, 1024, 128), F32),
            vmem((1024, 128), F32),
            vmem((2, 1024, 128), F32),
            vmem((512, 128), F32),
            vmem((512, 128), F32),
            vmem((1024, 128), F32),
            vmem((1024, 128), F32),
            vmem((8, 256), F32),
            vmem((2, 8, 256), F32),
            vmem((8, 1024), F32),
            vmem((8, 1024), F32),
            vmem((2, 2, 4, 512, 128), BF16),
            vmem((4, 1024, 256), BF16),
            vmem((2, 4, 512, 128), F32),
            vmem((4, 1024, 256), BF16),
            vmem((2, ROWS, 1024), BF16),
            vmem((ROWS, PIX), F32),
            vmem((BANKS, ROWS, PIX), BF16),
            dma(12), dma(15), dma(15), dma(15), dma(15), dma(2), dma(2), dma(4, 2), dma(4, 2),
            dma(4, 2), dma(4, 2), dma(4, 2), dma(4, 2), dma(4), dma(4), dma(4, 2), dma(4, 2),
            dma(4, 2), dma(4, 2), dma(5), dma(5), dma(9),
        ],
        compiler_params=pltpu.CompilerParams(
            collective_id=0, has_side_effects=True, vmem_limit_bytes=60 * 1024 * 1024
        ),
    )(
        image[0],
        dual_coeffs[:, 0],
        block_ids,
        block_counts,
        block_weights[0],
        block_data[0],
        *constants,
    )
    image_new, dual_new = pl.pallas_call(
        clip_kernel,
        out_shape=(
            jax.ShapeDtypeStruct((ROWS, PIX), F32),
            jax.ShapeDtypeStruct((BANKS, ROWS, PIX), BF16),
        ),
        in_specs=[in_hbm, in_hbm],
        out_specs=(in_hbm, in_hbm),
        scratch_shapes=[vmem((ROWS, PIX), F32), vmem((BANKS, ROWS, PIX), BF16), dma(8), dma(8)],
        compiler_params=pltpu.CompilerParams(vmem_limit_bytes=60 * 1024 * 1024),
    )(image_new, dual_new)
    return image_new[None], dual_new[:, None]


def solution(mesh):
    constants = tuple(jnp.asarray(c) for c in make_constants())

    def body(*args):
        return per_device(constants, *args)

    return jax.shard_map(
        body,
        mesh=mesh,
        in_specs=(
            P("chan", "strip", None),
            P(None, "chan", "strip", None),
            P("chan", "strip"),
            P("chan", "strip"),
            P("chan", "strip", None, None),
            P("chan", None, "strip", None, None),
        ),
        out_specs=(P("chan", "strip", None), P(None, "chan", "strip", None)),
        check_vma=False,
    )
```

```python
import math

import jax
import jax.numpy as jnp
import numpy as np
from jax import lax
from jax.experimental import pallas as pl
from jax.experimental.pallas import tpu as pltpu
from jax.sharding import PartitionSpec as P

MESH = pl.DeviceIdType.MESH
F32, BF16 = jnp.float32, jnp.bfloat16

PIX = 2048
ROWS = 128
STRIPS = 16
RIM = 8
PAD = ROWS + 2 * RIM
BANKS = 2
QUARTER = ROWS // 4
CHUNKS = 4
FAR_FIRST = [
    (dx, dy, core)
    for dx, dy in ((1, 2), (0, 2), (1, 1), (1, 3), (0, 1), (0, 3), (1, 0))
    for core in (0, 1)
] + [(0, 0, 1)]

root_three = math.sqrt(3.0)
sqrt_two = math.sqrt(2.0)
daub_two = [
    (1.0 + root_three) / (4.0 * sqrt_two),
    (3.0 + root_three) / (4.0 * sqrt_two),
    (3.0 - root_three) / (4.0 * sqrt_two),
    (1.0 - root_three) / (4.0 * sqrt_two),
]
daub_four = [
    0.2303778133088964,
    0.7148465705529155,
    0.6308807679298587,
    -0.0279837694168599,
    -0.1870348117190931,
    0.0308413818355607,
    0.0328830116668852,
    -0.010597401785069,
]
bank_filters = [daub_two, daub_four]
sigma_dual = 0.5
tau_primal = 0.3
shrink_level = 0.5


def bank_matrix(taps, out_at, out_count, in_at, in_count):
    count = len(taps)
    high = [(-1) ** k * taps[count - 1 - k] for k in range(count)]
    offset = count // 2 - 1
    matrix = np.zeros((out_count, in_count), np.float64)
    for i in range(out_count):
        m = out_at + i
        even = m - m % 2
        for k in range(count):
            n = even + k - offset - in_at
            if 0 <= n < in_count:
                matrix[i, n] = (taps if m % 2 == 0 else high)[k]
    return matrix


def make_constants():
    two_pi = 2.0 * math.pi
    tables = []
    for parity in range(2):
        tile, part, k = np.meshgrid(np.arange(8), np.arange(2), np.arange(64), indexing="ij")
        freq = 128 * tile + 2 * k + parity
        phase = part * (math.pi / 2)
        if parity == 0:
            freq[0, 1, 0] = PIX // 2
            phase = phase.copy()
            phase[0, 1, 0] = 0.0
        freq, phase = freq.reshape(-1), phase.reshape(-1)
        coarse = two_pi * (32 * np.arange(32)[:, None] * freq[None, :] % PIX) / PIX
        fine = two_pi * (np.arange(32)[:, None] * freq[None, :] % PIX) / PIX + phase[None, :]
        tables += [np.cos(coarse), np.sin(coarse), np.cos(fine) / 32.0, np.sin(fine) / 32.0]
    tables = np.stack(tables).astype(np.float32)
    grid = two_pi * (np.arange(512)[:, None] * np.arange(512)[None, :] % 512) / 512
    fourier = np.concatenate([np.cos(grid), np.sin(grid)], axis=1) / 64.0
    twiddle = np.zeros((512, 128), np.float32)
    for u in (1, 2, 3):
        angle = two_pi * (np.arange(512) * u) / PIX
        twiddle[:, 2 * u - 2] = np.cos(angle)
        twiddle[:, 2 * u - 1] = np.sin(angle)
    ana_cols = np.concatenate(
        [bank_matrix(t, 128, 128, 0, 384).T for t in bank_filters], axis=1
    )
    ana_rows = np.stack([sigma_dual * bank_matrix(t, RIM, ROWS, 0, PAD) for t in bank_filters])
    syn_all = np.stack([bank_matrix(t, 0, PAD, RIM, ROWS).T for t in bank_filters])
    syn_rows = syn_all[:, :, RIM : RIM + ROWS]
    rims = np.concatenate([syn_all[:, :, 0:RIM], syn_all[:, :, RIM + ROWS :]], axis=2)
    syn_rims = np.concatenate([rims[:, 0:16], rims[:, ROWS - 16 :]], axis=1)
    syn_cols = np.concatenate([bank_matrix(t, 0, 384, 128, 128) for t in bank_filters], axis=0)
    as_bf16 = lambda a: np.asarray(a, np.float32).astype(BF16)
    return (
        tables,
        as_bf16(fourier),
        twiddle,
        as_bf16(ana_cols),
        as_bf16(ana_rows),
        as_bf16(syn_rows),
        as_bf16(syn_rims),
        as_bf16(syn_cols),
    )


def dot(a, b):
    return jnp.dot(a, b, preferred_element_type=F32)


def lanes(shape):
    return lax.broadcasted_iota(jnp.int32, shape, len(shape) - 1)


def loop(count, body):
    def step(i, carry):
        body(i)
        return carry

    lax.fori_loop(0, count, step, 0)


def peer_at(me, k):
    dx, dy, core = FAR_FIRST[k]
    return ((me // 8 + dx) % 2) * 8 + (((me // 2) % 4 + dy) % 4) * 2 + (me + core) % 2


def at(i, width):
    return pl.ds(pl.multiple_of(i * width, width), width)


def kernel(
    image_hbm, dual_hbm, ids_hbm, counts_hbm, weights_hbm, data_hbm,
    tables_hbm, fourier_hbm, twiddle_hbm, ana_cols_hbm, ana_rows_hbm, syn_rows_hbm, syn_rims_hbm, syn_cols_hbm,
    image_out, dual_out,
    ids_ref, counts_ref, xpad, xwide, dual, weights, data, tables, fourier, twiddle, ana_cols, ana_rows, syn_rows, syn_rims, syn_cols,
    basis, folded, ysend, yrecv, hsend, hrecv, coeffs, trial, squares, near, far, quarter_sum, other_sum,
    factor, combined, edge_send, edge_recv, synth_wide, adjoint, own_flat, other_flat, rim_flat,
    w_send, w_recv, d_send, d_recv, ids_send, ids_recv, rim_send, rim_recv, wd_dense,
    forward, kept, backward, packed, image_new, dual_new,
    local_sem, y_s, y_r, h_s, h_r, halo_s, halo_r, edge_s, edge_r, far_s, far_r, near_s, near_r,
    x_s, x_r, ga_s, ga_r, gb_s, gb_r, swap_s, swap_r, out_sem,
):
    me = lax.axis_index("strip")
    chan = lax.axis_index("chan")
    z = chan % 4
    x_hi = chan // 4
    zp, zm, zf = (z + 1) % 4, (z + 3) % 4, (z + 2) % 4
    up = {"chan": x_hi * 4 + zp}
    down = {"chan": x_hi * 4 + zm}
    across = {"chan": (1 - x_hi) * 4 + z}
    before, after = {"strip": (me + 15) % STRIPS}, {"strip": (me + 1) % STRIPS}
    sign = jnp.where(me < 8, 1, -1)

    sources = {
        "ids": (ids_hbm, ids_ref),
        "counts": (counts_hbm, counts_ref),
        "weights": (weights_hbm, weights),
        "data": (data_hbm, data),
        "image": (image_hbm, xpad.at[RIM : RIM + ROWS]),
        "tables": (tables_hbm, tables),
        "ana_cols": (ana_cols_hbm, ana_cols),
        "ana_rows": (ana_rows_hbm, ana_rows),
        "dual": (dual_hbm, dual),
        "fourier": (fourier_hbm, fourier),
        "twiddle": (twiddle_hbm, twiddle),
        "syn_rows": (syn_rows_hbm, syn_rows),
        "syn_rims": (syn_rims_hbm, syn_rims),
        "syn_cols": (syn_cols_hbm, syn_cols),
    }
    loads = {
        name: pltpu.make_async_copy(src, dst, local_sem.at[i])
        for i, (name, (src, dst)) in enumerate(sources.items())
    }
    for load in loads.values():
        load.start()

    barrier = pltpu.get_barrier_semaphore()
    for k in range(1, STRIPS):
        pl.semaphore_signal(
            barrier, inc=1, device_id={"strip": (me + k) % STRIPS}, device_id_type=MESH
        )
    for peer in (up, down, across):
        pl.semaphore_signal(barrier, inc=1, device_id=peer, device_id_type=MESH)
    def remote(src, dst, send, recv, peer):
        return pltpu.make_async_remote_copy(
            src_ref=src, dst_ref=dst, send_sem=send, recv_sem=recv, device_id=peer, device_id_type=MESH
        )

    loads["weights"].wait()
    loads["data"].wait()
    lane_of = lanes((128, 128))
    half_lane = lane_of % 64
    imag_lane = lane_of >= 64
    column_row = lax.broadcasted_iota(jnp.int32, (128, 128), 0)
    own_hit = column_row == jnp.where(me < 8, 2 * half_lane, 127 - 2 * half_lane)
    other_hit = column_row == jnp.where(me < 8, 2 * half_lane + 1, 128 - 2 * half_lane)
    one_hot = lambda mask: jnp.where(mask, 1.0, 0.0).astype(BF16)
    signed = lambda mask: jnp.where(mask, sign.astype(F32), 0.0).astype(BF16)
    own_real, own_imag = one_hot(own_hit & ~imag_lane), signed(own_hit & imag_lane)
    other_real, other_imag = one_hot(other_hit & ~imag_lane), signed(other_hit & imag_lane)
    other_low, other_high = one_hot(other_hit & ~imag_lane), one_hot(other_hit & imag_lane)
    mirror = {"strip": 15 - me}
    rim_peer = {"strip": jnp.where(me < 8, 8 + (8 - me) % 8, (16 - me) % 8)}

    def picked_rows(ref, i):
        return ref[8 * i : 8 * i + 8].reshape(256, 128)

    for i in range(4):
        rows = slice(256 * i, 256 * i + 256)
        d_send[rows, :] = dot(picked_rows(data.at[0], i), other_real) + dot(
            picked_rows(data.at[1], i), other_imag
        )
        if i < 2:
            w_send[rows, :] = dot(picked_rows(weights, i), other_low) + dot(
                picked_rows(weights, i + 2), other_high
            )
    loads["ids"].wait()
    loads["counts"].wait()
    slot = lanes((8, 32))
    ids = jnp.broadcast_to(ids_ref[...], (8, 32))
    live_ids = jnp.where(slot < counts_ref[...], ids, -1).astype(F32).astype(BF16)
    spread = jnp.where(
        lanes((32, 256)) // 8 == lax.broadcasted_iota(jnp.int32, (32, 256), 0), 1.0, 0.0
    ).astype(BF16)
    ids_send[...] = dot(live_ids, spread)
    sel_row, sel_lane = lax.broadcasted_iota(jnp.int32, (8, 128), 0), lanes((8, 128))
    turn = (((1,), (1,)), ((), ()))
    rim = 0.0
    for i, values in enumerate((weights[...], data[0], data[1])):
        select = one_hot((sel_row == i) & (sel_lane == 0))
        rim = rim + lax.dot_general(select, values.reshape(1024, 128), turn, preferred_element_type=F32)
    rim_send[...] = rim
    pl.semaphore_wait(barrier, STRIPS + 2)

    halos = [
        remote(xpad.at[RIM : 2 * RIM], xpad.at[RIM + ROWS : PAD], halo_s.at[0], halo_r.at[0], before),
        remote(xpad.at[ROWS : RIM + ROWS], xpad.at[0:RIM], halo_s.at[1], halo_r.at[1], after),
    ]
    loads["image"].wait()
    for copy in halos:
        copy.start()
    swaps = [
        remote(w_send, w_recv, swap_s.at[0], swap_r.at[0], mirror),
        remote(ids_send, ids_recv.at[0], swap_s.at[1], swap_r.at[1], mirror),
        remote(ids_send, ids_recv.at[1], swap_s.at[2], swap_r.at[2], rim_peer),
        remote(rim_send, rim_recv, swap_s.at[3], swap_r.at[3], rim_peer),
        remote(d_send, d_recv, swap_s.at[4], swap_r.at[4], mirror),
    ]
    for copy in swaps:
        copy.start()

    loads["tables"].wait()
    for parity in range(2):
        def make_basis(i, parity=parity):
            coarse_cos = tables[4 * parity, pl.ds(i, 1), :]
            coarse_sin = tables[4 * parity + 1, pl.ds(i, 1), :]
            block = coarse_cos * tables[4 * parity + 2] - coarse_sin * tables[4 * parity + 3]
            basis[parity, at(i, 32), :] = block.astype(BF16)

        loop(32, make_basis)
    left, right = xpad[RIM : RIM + ROWS, 0:1024], xpad[RIM : RIM + ROWS, 1024:2048]
    folded[0] = (left + right).astype(BF16)
    folded[1] = (left - right).astype(BF16)
    def y_copy(k):
        q = peer_at(me, k)
        return remote(ysend.at[q], yrecv.at[at(me, ROWS)], y_s.at[k], y_r.at[k], {"strip": q})

    for e in range(2):
        for pair in range(4):
            tiles = dot(folded[e], basis[e, :, 256 * pair : 256 * pair + 256])
            for half in range(2):
                p = 2 * pair + half
                ysend[15 - p if e else p] = tiles[:, 128 * half : 128 * half + 128]
    for k in range(15):
        y_copy(k).start()
    yrecv[at(me, ROWS), :] = ysend[me]

    for copy in halos:
        copy.wait_recv()
    for name in ("ana_cols", "ana_rows", "dual"):
        loads[name].wait()
    xwide[:, 0:128] = jnp.zeros((PAD, 128), BF16)
    xwide[:, 128 + PIX : 256 + PIX] = jnp.zeros((PAD, 128), BF16)
    row = lax.broadcasted_iota(jnp.int32, (PAD, PIX), 0)
    outside = ((row < RIM) & (me == 0)) | ((row >= RIM + ROWS) & (me == STRIPS - 1))
    xwide[:, 128 : 128 + PIX] = jnp.where(outside, 0.0, xpad[...]).astype(BF16)

    def analyse_columns(i):
        for t in range(4):
            start = pl.multiple_of(i * 512 + t * 128, 128)
            both = dot(xwide[:, pl.ds(start, 384)], ana_cols[...]).astype(BF16)
            coeffs[0, :, pl.ds(start, 128)] = both[:, 0:128]
            coeffs[1, :, pl.ds(start, 128)] = both[:, 128:256]

    loop(4, analyse_columns)

    def cols_of(c):
        return slice(1024 * (c % 2), 1024 * (c % 2) + 1024)

    def far_copies(c):
        bank, cols = c // 2, cols_of(c)
        low = pl.ds(pl.multiple_of(zf * QUARTER, QUARTER), 16)
        high = pl.ds(pl.multiple_of(zf * QUARTER + 16, 16), 16)
        return [
            remote(squares.at[bank, low, cols], far.at[bank, 0, :, cols], far_s.at[c, 0], far_r.at[c, 0], up),
            remote(squares.at[bank, high, cols], far.at[bank, 1, :, cols], far_s.at[c, 1], far_r.at[c, 1], down),
        ]

    def near_copies(c):
        bank, cols = c // 2, cols_of(c)
        return [
            remote(
                squares.at[bank, at(where, QUARTER), cols], near.at[bank, side, :, cols],
                near_s.at[c, side], near_r.at[c, side], peer,
            )
            for side, (where, peer) in enumerate(((zp, up), (zm, down)))
        ]

    def x_copy(c):
        bank, cols = c // 2, cols_of(c)
        return remote(
            quarter_sum.at[bank, :, cols], other_sum.at[bank, :, cols], x_s.at[c], x_r.at[c], across
        )

    def gather_near(c):
        mine = factor.at[c // 2, at(z, QUARTER), cols_of(c)]
        return [
            remote(mine, mine, ga_s.at[c, side], ga_r.at[c, side], peer)
            for side, peer in enumerate((up, down))
        ]

    def gather_far(c):
        low = factor.at[c // 2, pl.ds(pl.multiple_of(zm * QUARTER, QUARTER), 16), cols_of(c)]
        high = factor.at[c // 2, pl.ds(pl.multiple_of(zp * QUARTER + 16, 16), 16), cols_of(c)]
        return [
            remote(low, low, gb_s.at[c, 0], gb_r.at[c, 0], up),
            remote(high, high, gb_s.at[c, 1], gb_r.at[c, 1], down),
        ]

    def edge_copies(c):
        cols = cols_of(c)
        return [
            remote(
                edge_send.at[c // 2, side, :, cols], edge_recv.at[c // 2, side, :, cols],
                edge_s.at[c, side], edge_r.at[c, side], peer,
            )
            for side, peer in enumerate((before, after))
        ]

    for c in range(CHUNKS):
        bank = c // 2
        for t in range(4):
            cols = slice(1024 * (c % 2) + 256 * t, 1024 * (c % 2) + 256 * t + 256)
            values = dual[bank, :, cols].astype(F32) + dot(ana_rows[bank], coeffs[bank, :, cols])
            trial[bank, :, cols] = values
            squares[bank, :, cols] = values * values
        for copy in far_copies(c):
            copy.start()

    for i in range(4):
        rows = slice(256 * i, 256 * i + 256)
        own_flat[0, rows, :] = dot(picked_rows(weights, i), one_hot(own_hit))
        own_flat[1, rows, :] = dot(picked_rows(data.at[0], i), own_real) + dot(
            picked_rows(data.at[1], i), own_imag
        )
    place_row = lax.broadcasted_iota(jnp.int32, (512, 256), 0)
    same_row = place_row % 8 == lanes((512, 256)) % 8

    def place_of(slot_ids):
        return one_hot((slot_ids[0:1, :].astype(jnp.int32) == place_row // 8) & same_row)

    def by_row(flat_w, flat_d, u):
        rows = pl.ds(u, 256, stride=4)
        return jnp.concatenate([flat_w[rows, :], flat_d[rows, :]], axis=1).astype(BF16)

    def put_dense(role, u, values):
        values = values.astype(BF16)
        wd_dense[role, 0, u] = values[:, 0:128]
        wd_dense[role, 1, u] = values[:, 128:256]

    own_place = place_of(ids_send[...])
    for u in range(4):
        put_dense(0, u, dot(own_place, by_row(own_flat.at[0], own_flat.at[1], u)))

    lane_sign = jnp.where(lanes((1, 128)) < 64, -sign, sign).astype(F32)
    swap_halves = lambda values: pltpu.roll(values, 64, 1)
    first_lane = (lanes((1, 128)) == 0) & (me == 0)
    middle_lane = (lanes((1, 128)) == 64) & (me == 0)

    def times_i(values):
        return lane_sign * swap_halves(values)

    def h_copy(k):
        q = peer_at(me, k)
        return remote(hsend.at[at(q, ROWS)], hrecv.at[me], h_s.at[k], h_r.at[k], {"strip": q})

    def fold_rows(i):
        for part in range(2):
            start = i * 128 + part * 64
            rows = pl.ds(pl.multiple_of(start, 64), 64)
            low = pl.ds(pl.multiple_of(512 + start, 64), 64)
            loaded = [yrecv[pl.ds(pl.multiple_of(512 * j + start, 64), 64), :] for j in range(4)]
            tw = twiddle[rows, :]
            for role in range(2):
                if role == 0:
                    parts = [jnp.where(middle_lane, 0.0, y) for y in loaded]
                else:
                    parts = [
                        jnp.where(first_lane, swap_halves(y), jnp.where(middle_lane, 0.0, y)) for y in loaded
                    ]
                unit = times_i if role == 0 else (lambda values: -times_i(values))
                y0, y1, y2, y3 = parts
                sum_a, sum_b, dif_a, dif_b = y0 + y2, y1 + y3, y0 - y2, y1 - y3
                total, alt = sum_a + sum_b, sum_a - sum_b
                turned_a, turned_b = unit(dif_a), unit(dif_b)
                folds = (
                    (total, unit(total)),
                    (dif_a - turned_b, turned_a + dif_b),
                    (alt, unit(alt)),
                    (dif_a + turned_b, turned_a - dif_b),
                )
                lanes_of = slice(128 * role, 128 * role + 128)
                for u, (value, turned) in enumerate(folds):
                    if u > 0:
                        cos, sin = tw[:, 2 * u - 2 : 2 * u - 1], tw[:, 2 * u - 1 : 2 * u]
                        value, turned = cos * value - sin * turned, cos * turned + sin * value
                    forward[u, rows, lanes_of] = value.astype(BF16)
                    forward[u, low, lanes_of] = (-turned).astype(BF16)

    def weigh(role, u, rows, spectrum):
        weight = wd_dense[role, 0, u, rows, :].astype(F32)
        return weight * (weight * spectrum - wd_dense[role, 1, u, rows, :].astype(F32))

    def transform_columns():
        for k in range(15):
            y_copy(k).wait_recv()
        loop(4, fold_rows)
        for u in range(4):
            for m in range(2):
                rows = slice(256 * m, 256 * m + 256)
                both = dot(fourier[rows, :], forward[u])
                kept[0, u, rows, :] = weigh(0, u, rows, both[:, 0:128])
                kept[1, u, rows, :] = both[:, 128:256]

    def receive_swaps():
        for copy in swaps:
            copy.wait_recv()
        for m in range(2):
            rows = slice(256 * m, 256 * m + 256)
            values = w_recv[rows, :]
            turned = swap_halves(values)
            left_lane = lanes((256, 128)) < 64
            other_flat[256 * m : 256 * m + 256, :] = jnp.where(left_lane, values, turned)
            other_flat[512 + 256 * m : 768 + 256 * m, :] = jnp.where(left_lane, turned, values)
        rims = jnp.concatenate([rim_recv[...], jnp.zeros((120, 1024), F32)], axis=0).T.astype(BF16)
        has_rim = me < 8
        rim_w = one_hot((column_row == 0) & (half_lane == 0) & has_rim)
        rim_d = one_hot((column_row == 1) & (lane_of == 0) & has_rim) - one_hot(
            (column_row == 2) & (lane_of == 64) & has_rim
        )
        rim_flat[0] = dot(rims, rim_w)
        rim_flat[1] = dot(rims, rim_d)
        other_place, rim_place = place_of(ids_recv[0]), place_of(ids_recv[1])
        for u in range(4):
            put_dense(
                1, u,
                dot(other_place, by_row(other_flat, d_recv, u))
                + dot(rim_place, by_row(rim_flat.at[0], rim_flat.at[1], u)),
            )

    def transform_back():
        for u in range(4):
            for m in range(2):
                rows, low = slice(256 * m, 256 * m + 256), slice(512 + 256 * m, 768 + 256 * m)
                own, other = kept[0, u, rows, :], weigh(1, u, rows, kept[1, u, rows, :])
                own_turned, other_swapped = times_i(own), swap_halves(other)
                value = jnp.where(first_lane, own, jnp.where(middle_lane, other_swapped, own + other))
                turned = jnp.where(
                    first_lane, own_turned,
                    jnp.where(middle_lane, other, own_turned - lane_sign * other_swapped),
                )
                value, turned = value.astype(BF16), turned.astype(BF16)
                backward[u, rows, 0:128] = value
                backward[u, low, 0:128] = turned
                if u > 0:
                    backward[u, rows, 128:256] = turned
                    backward[u, low, 128:256] = -value
        for m in range(4):
            rows = slice(128 * m, 128 * m + 128)
            left_side = fourier[rows, :]
            tw = twiddle[rows, :]
            terms = [dot(left_side, backward[0, :, 0:128])]
            for u in (1, 2, 3):
                both = dot(left_side, backward[u])
                cos, sin = tw[:, 2 * u - 2 : 2 * u - 1], tw[:, 2 * u - 1 : 2 * u]
                value, turned = both[:, 0:128], both[:, 128:256]
                terms.append(cos * value + sin * turned)
                if u == 1:
                    turned_odd = cos * turned - sin * value
                if u == 3:
                    turned_odd = turned_odd - (cos * turned - sin * value)
            plus, minus, odd = terms[0] + terms[2], terms[0] - terms[2], terms[1] + terms[3]
            for j, value in enumerate((plus + odd, minus + turned_odd, plus - odd, minus - turned_odd)):
                hsend[512 * j + 128 * m : 512 * j + 128 * m + 128, :] = value
        for k in range(15):
            h_copy(k).start()
        hrecv[me] = hsend[at(me, ROWS), :]

    def send_near(c):
        bank, cols = c // 2, cols_of(c)
        for copy in far_copies(c):
            copy.wait_recv()
        low = pl.ds(pl.multiple_of(zp * QUARTER, QUARTER), 16)
        high = pl.ds(pl.multiple_of(zm * QUARTER + 16, 16), 16)
        squares[bank, low, cols] = squares[bank, low, cols] + far[bank, 0, :, cols]
        squares[bank, high, cols] = squares[bank, high, cols] + far[bank, 1, :, cols]
        for copy in near_copies(c):
            copy.start()

    def send_across(c):
        bank, cols = c // 2, cols_of(c)
        for copy in near_copies(c):
            copy.wait_recv()
        quarter_sum[bank, :, cols] = (
            squares[bank, at(z, QUARTER), cols] + near[bank, 0, :, cols] + near[bank, 1, :, cols]
        )
        x_copy(c).start()

    bound = shrink_level * math.sqrt(8.0)

    def send_factor(c):
        bank, cols = c // 2, cols_of(c)
        x_copy(c).wait_recv()
        total = quarter_sum[bank, :, cols] + other_sum[bank, :, cols]
        factor[bank, at(z, QUARTER), cols] = bound / jnp.maximum(jnp.sqrt(total), bound)
        for copy in gather_near(c):
            copy.start()

    def pass_factor(c):
        for copy in gather_near(c):
            copy.wait_recv()
        for copy in gather_far(c):
            copy.start()

    def shrink(c):
        bank, cols = c // 2, cols_of(c)
        for copy in gather_far(c):
            copy.wait_recv()
        for i in range(8):
            rows = slice(16 * i, 16 * i + 16)
            fresh = (trial[bank, rows, cols] * factor[bank, rows, cols]).astype(BF16)
            dual_new[bank, rows, cols] = fresh
            values = 2.0 * fresh.astype(F32) - dual[bank, rows, cols].astype(F32)
            combined[bank, rows, cols] = values.astype(BF16)
            if i == 0:
                edge_send[bank, 0, :, cols] = values[0:RIM]
            if i == 7:
                edge_send[bank, 1, :, cols] = values[16 - RIM : 16]
        for copy in edge_copies(c):
            copy.start()

    def synthesise_rows(c):
        bank = c // 2
        for t in range(4):
            start = 1024 * (c % 2) + 256 * t
            values = dot(syn_rows[bank], combined[bank, :, start : start + 256])
            synth_wide[bank, :, 128 + start : 384 + start] = values.astype(BF16)

    def add_edges(c):
        bank, cols = c // 2, cols_of(c)
        wide = slice(128 + 1024 * (c % 2), 1152 + 1024 * (c % 2))
        for copy in edge_copies(c):
            copy.wait_recv()
        below = jnp.where(me == STRIPS - 1, 0.0, edge_recv[bank, 0, :, cols])
        above = jnp.where(me == 0, 0.0, edge_recv[bank, 1, :, cols])
        extra = dot(syn_rims[bank], jnp.concatenate([above, below], axis=0).astype(BF16))
        for rows, part in ((slice(0, 16), extra[0:16]), (slice(ROWS - 16, ROWS), extra[16:32])):
            synth_wide[bank, rows, wide] = (synth_wide[bank, rows, wide].astype(F32) + part).astype(BF16)

    def synthesise_columns(i, rows):
        for t in range(4):
            start = pl.multiple_of(i * 512 + t * 128, 128)
            window = pl.ds(start, 384)
            adjoint[rows, pl.ds(start, 128)] = dot(synth_wide[0, rows, window], syn_cols[0:384]) + dot(
                synth_wide[1, rows, window], syn_cols[384:768]
            )

    inner, outer = slice(16, ROWS - 16), (slice(0, 16), slice(ROWS - 16, ROWS))

    for c in range(CHUNKS):
        send_near(c)
    for name in ("fourier", "twiddle", "syn_rows", "syn_rims", "syn_cols"):
        loads[name].wait()
    for bank in range(BANKS):
        synth_wide[bank, :, 0:128] = jnp.zeros((ROWS, 128), BF16)
        synth_wide[bank, :, 128 + PIX : 256 + PIX] = jnp.zeros((ROWS, 128), BF16)
    send_across(0)
    send_across(1)
    send_across(2)
    send_across(3)
    transform_columns()
    send_factor(0)
    send_factor(1)
    send_factor(2)
    receive_swaps()
    transform_back()
    send_factor(3)
    pass_factor(0)
    pass_factor(1)
    pass_factor(2)
    pass_factor(3)
    shrink(0)
    synthesise_rows(0)
    shrink(1)
    synthesise_rows(1)
    shrink(2)
    synthesise_rows(2)
    shrink(3)
    synthesise_rows(3)
    dual_copy = pltpu.make_async_copy(dual_new, dual_out, out_sem.at[0])
    dual_copy.start()
    loop(4, lambda i: synthesise_columns(i, inner))
    for c in range(CHUNKS):
        add_edges(c)
    loop(4, lambda i: [synthesise_columns(i, rows) for rows in outer])

    for k in range(15):
        h_copy(k).wait_recv()
    for p in range(8):
        packed[0, :, 128 * p : 128 * p + 128] = hrecv[p].astype(BF16)
        packed[1, :, 128 * p : 128 * p + 128] = hrecv[15 - p].astype(BF16)

    def finish(i):
        cols = at(i, 256)
        even, odd = (
            lax.dot_general(packed[j], basis[j, cols, :], turn, preferred_element_type=F32)
            for j in range(2)
        )
        for gradient, where in (
            (even + odd, cols),
            (even - odd, pl.ds(pl.multiple_of(1024 + i * 256, 256), 256)),
        ):
            image_new[:, where] = xpad[RIM : RIM + ROWS, where] - tau_primal * (
                gradient + adjoint[:, where]
            )

    def image_copies(i):
        return [
            pltpu.make_async_copy(image_new.at[:, cols], image_out.at[:, cols], out_sem.at[1 + 2 * i + side])
            for side, cols in enumerate(
                (at(i, 256), pl.ds(pl.multiple_of(1024 + i * 256, 256), 256))
            )
        ]

    def finish_and_send(i):
        finish(i)
        for copy in image_copies(i):
            copy.start()

    loop(4, finish_and_send)

    for copy in halos:
        copy.wait_send()
    for k in range(15):
        y_copy(k).wait_send()
        h_copy(k).wait_send()
    for copy in swaps:
        copy.wait_send()
    for c in range(CHUNKS):
        for copy in far_copies(c) + near_copies(c) + gather_near(c) + gather_far(c) + edge_copies(c):
            copy.wait_send()
        x_copy(c).wait_send()
    dual_copy.wait()
    for i in range(4):
        for copy in image_copies(i):
            copy.wait()


def clip_kernel(image_hbm, dual_hbm, image_out, dual_out, image, dual, in_sem, out_sem):
    parts = [
        (image_hbm.at[32 * i : 32 * i + 32], image.at[32 * i : 32 * i + 32], image_out.at[32 * i : 32 * i + 32])
        for i in range(4)
    ] + [
        (dual_hbm.at[b, 64 * i : 64 * i + 64], dual.at[b, 64 * i : 64 * i + 64], dual_out.at[b, 64 * i : 64 * i + 64])
        for b in range(2)
        for i in range(2)
    ]
    reads = [pltpu.make_async_copy(p[0], p[1], in_sem.at[i]) for i, p in enumerate(parts)]
    writes = [pltpu.make_async_copy(p[1], p[2], out_sem.at[i]) for i, p in enumerate(parts)]
    for read in reads:
        read.start()
    for i, (read, write) in enumerate(zip(reads, writes)):
        read.wait()
        if i < 4:
            image[32 * i : 32 * i + 32] = jnp.maximum(image[32 * i : 32 * i + 32], 0.0)
        write.start()
    for write in writes:
        write.wait()


def per_device(constants, image, dual_coeffs, block_ids, block_counts, block_weights, block_data):
    any_space = in_hbm = pl.BlockSpec(memory_space=pl.ANY)
    dma = lambda *n: pltpu.SemaphoreType.DMA(n)
    vmem = pltpu.VMEM
    image_new, dual_new = pl.pallas_call(
        kernel,
        out_shape=(
            jax.ShapeDtypeStruct((ROWS, PIX), F32),
            jax.ShapeDtypeStruct((BANKS, ROWS, PIX), BF16),
        ),
        in_specs=[any_space] * 4 + [any_space] * 10,
        out_specs=(any_space, any_space),
        scratch_shapes=[
            vmem((1, 32), jnp.int32),
            vmem((1, 1), jnp.int32),
            vmem((PAD, PIX), F32),
            vmem((PAD, PIX + 256), BF16),
            vmem((BANKS, ROWS, PIX), BF16),
            vmem((32, 32, 128), BF16),
            vmem((2, 32, 32, 128), BF16),
            vmem((8, 32, 1024), F32),
            vmem((512, 1024), BF16),
            vmem((512, 128), F32),
            vmem((384, 256), BF16),
            vmem((BANKS, ROWS, PAD), BF16),
            vmem((BANKS, ROWS, ROWS), BF16),
            vmem((BANKS, 32, 2 * RIM), BF16),
            vmem((768, 128), BF16),
            vmem((2, 1024, 1024), BF16),
            vmem((2, ROWS, 1024), BF16),
            vmem((STRIPS, ROWS, 128), F32),
            vmem((PIX, 128), F32),
            vmem((PIX, 128), F32),
            vmem((STRIPS, ROWS, 128), F32),
            vmem((BANKS, PAD, PIX), BF16),
            vmem((BANKS, ROWS, PIX), F32),
            vmem((BANKS, ROWS, PIX), F32),
            vmem((BANKS, 2, QUARTER, PIX), F32),
            vmem((BANKS, 2, 16, PIX), F32),
            vmem((BANKS, QUARTER, PIX), F32),
            vmem((BANKS, QUARTER, PIX), F32),
            vmem((BANKS, ROWS, PIX), F32),
            vmem((BANKS, ROWS, PIX), BF16),
            vmem((BANKS, 2, RIM, PIX), F32),
            vmem((BANKS, 2, RIM, PIX), F32),
            vmem((BANKS, ROWS, PIX + 256), BF16),
            vmem((ROWS, PIX), F32),
            vmem((2, 1024, 128), F32),
            vmem((1024, 128), F32),
            vmem((2, 1024, 128), F32),
            vmem((512, 128), F32),
            vmem((512, 128), F32),
            vmem((1024, 128), F32),
            vmem((1024, 128), F32),
            vmem((8, 256), F32),
            vmem((2, 8, 256), F32),
            vmem((8, 1024), F32),
            vmem((8, 1024), F32),
            vmem((2, 2, 4, 512, 128), BF16),
            vmem((4, 1024, 256), BF16),
            vmem((2, 4, 512, 128), F32),
            vmem((4, 1024, 256), BF16),
            vmem((2, ROWS, 1024), BF16),
            vmem((ROWS, PIX), F32),
            vmem((BANKS, ROWS, PIX), BF16),
            dma(14), dma(15), dma(15), dma(15), dma(15), dma(2), dma(2), dma(4, 2), dma(4, 2),
            dma(4, 2), dma(4, 2), dma(4, 2), dma(4, 2), dma(4), dma(4), dma(4, 2), dma(4, 2),
            dma(4, 2), dma(4, 2), dma(5), dma(5), dma(9),
        ],
        compiler_params=pltpu.CompilerParams(
            collective_id=0, has_side_effects=True, vmem_limit_bytes=60 * 1024 * 1024
        ),
    )(
        image[0],
        dual_coeffs[:, 0],
        block_ids,
        block_counts,
        block_weights[0],
        block_data[0],
        *constants,
    )
    image_new, dual_new = pl.pallas_call(
        clip_kernel,
        out_shape=(
            jax.ShapeDtypeStruct((ROWS, PIX), F32),
            jax.ShapeDtypeStruct((BANKS, ROWS, PIX), BF16),
        ),
        in_specs=[in_hbm, in_hbm],
        out_specs=(in_hbm, in_hbm),
        scratch_shapes=[vmem((ROWS, PIX), F32), vmem((BANKS, ROWS, PIX), BF16), dma(8), dma(8)],
        compiler_params=pltpu.CompilerParams(vmem_limit_bytes=60 * 1024 * 1024),
    )(image_new, dual_new)
    return image_new[None], dual_new[:, None]


def solution(mesh):
    constants = tuple(jnp.asarray(c) for c in make_constants())

    def body(*args):
        return per_device(constants, *args)

    return jax.shard_map(
        body,
        mesh=mesh,
        in_specs=(
            P("chan", "strip", None),
            P(None, "chan", "strip", None),
            P("chan", "strip"),
            P("chan", "strip"),
            P("chan", "strip", None, None),
            P("chan", None, "strip", None, None),
        ),
        out_specs=(P("chan", "strip", None), P(None, "chan", "strip", None)),
        check_vma=False,
    )
```
